256 devices in a mesh: grp: 4 (over x), tile: 64 (over z, y, core).
Axes of the slice: x: 4, y: 4, z: 8, core: 2. Of those that a mesh axis runs over, the one named last changes fastest.
Arguments:
- bricks: float32 [512, 128, 512], P(('grp', 'tile')), may hold values from 0 to 1
- colour_table: float32 [3, 256], replicated, may hold values from 0.5 to 8
- opacity_table: float32 [256], replicated, may hold values from 2e-05 to 0.005
- depth_order: int32 [4, 64], replicated, may hold values from 0 to 63, each once within a row
Outputs:
- image: float32 [4, 65536], P(None, ('grp', 'tile'))
The draws below stay inside these ranges and needn't reach their ends.
Inputs may be any that keep to these rules, and one draw needn't show every extreme that they name: Each row of depth_order holds every number 0 .. 63 once.
All inputs are finite; a program needn't handle non-finite values.
Results may differ from the reference program's by a relative error of at most 0.0003.
Values sent between devices are 32-bit elements; how exact they have to be, the bound alone decides.
A program may use at most 64 MiB of HBM per device.

```python
import math
import jax
import jax.numpy as jnp
from jax import lax

PIX = 512
KNOTS = 256
ROWS = 128
DEP = 2
GROUPS = 4
MEMBERS = 64
BRICKS = 256


def block_levels(rng, extent, pieces, smallest, high):
    def one(axis_at, shards_of):
        steps = jax.random.uniform(jax.random.fold_in(jax.random.fold_in(rng, 6), axis_at), (shards_of,), jnp.float32, smallest / len(pieces), high / len(pieces))
        return jnp.repeat(jnp.exp(steps), extent[axis_at] // shards_of).reshape((-1,) + (1,) * (len(extent) - axis_at - 1))

    factor_of = one(*pieces[0])
    for cut in pieces[1:]:
        factor_of = factor_of * one(*cut)
    return factor_of


def setup_inputs(seed: int = 0) -> dict:
    arg_keys = jax.random.split(jax.random.key(seed), 5)
    bricks = jnp.clip(1.0 * jax.random.uniform(arg_keys[0], (BRICKS * DEP, ROWS, PIX), jnp.float32) ** block_levels(arg_keys[0], (BRICKS * DEP, ROWS, PIX), ((0, 256),), -0.2, 0.2), 0.0, 1.0)
    colour_table = jnp.clip(jax.random.uniform(arg_keys[1], (3, KNOTS), jnp.float32, 0.5, 8.0), 0.5, 8.0)
    opacity_table = jnp.clip(jnp.exp(jax.random.uniform(arg_keys[2], (KNOTS,), jnp.float32, math.log(1.9999999494757503e-05), math.log(0.005))), 1.9999999494757503e-05, 0.005)
    depth_order = jax.vmap(lambda own: jax.random.permutation(own, MEMBERS))(jax.random.split(arg_keys[3], GROUPS)).reshape((GROUPS, MEMBERS)).astype(jnp.int32)
    return dict(bricks=bricks, colour_table=colour_table, opacity_table=opacity_table, depth_order=depth_order)


def reference(bricks, colour_table, opacity_table, depth_order):
    knot_count = opacity_table.shape[0]
    palette = jnp.concatenate([colour_table, opacity_table[None, :]], axis=0)
    volume = bricks.reshape(GROUPS * MEMBERS, DEP, ROWS * PIX)

    def one_brick(slab):
        def one_slice(carry, values):
            colour, transmit = carry
            position = values * (knot_count - 1)
            lower = jnp.clip(jnp.floor(position), 0, knot_count - 2)
            fraction = position - lower
            index_low = lower.astype(jnp.int32)
            sample = palette[:, index_low] * (1.0 - fraction) + palette[:, index_low + 1] * fraction
            weight = transmit * sample[3]
            colour = colour + weight[None, :] * sample[:3]
            transmit = transmit * (1.0 - sample[3])
            return (colour, transmit), None

        start = (jnp.zeros((3, ROWS * PIX), jnp.float32), jnp.ones((ROWS * PIX,), jnp.float32))
        (colour, transmit), unused = lax.scan(one_slice, start, slab)
        return jnp.concatenate([colour, (1.0 - transmit)[None, :]], axis=0)

    partials = lax.map(one_brick, volume)
    by_rank = jnp.argsort(depth_order, axis=1).astype(jnp.int32)
    sequence = (jnp.arange(GROUPS, dtype=jnp.int32)[:, None] * MEMBERS + by_rank).reshape(-1)

    def blend(picture, brick_id):
        return picture + (1.0 - picture[3:4]) * partials[brick_id], None

    picture, unused = lax.scan(blend, jnp.zeros((4, ROWS * PIX), jnp.float32), sequence)
    return picture
```

```python
import jax
import jax.numpy as jnp
from jax import lax
from jax.experimental import pallas as pl
from jax.experimental.pallas import tpu as pltpu
from jax.sharding import PartitionSpec as P

LANES = 128
ROWS_PER_STEP = 8


def lookup_tables(palette):
    channels, knots = palette.shape
    extended = jnp.concatenate([palette, palette[:, -1:]], axis=1)
    halves = knots // LANES
    lower = extended[:, 0:knots].reshape(channels, halves, LANES)
    upper = extended[:, 1 : knots + 1].reshape(channels, halves, LANES)
    tables = jnp.stack([lower, upper], axis=1)
    tables = jnp.broadcast_to(tables[..., None, :], (channels, 2, halves, ROWS_PER_STEP, LANES))
    return tables.reshape(channels * 2 * halves, ROWS_PER_STEP, LANES)


def shade_kernel(knots, values_ref, tables_ref, out_ref):
    channels = out_ref.shape[0]
    bricks = values_ref.shape[1]
    width = values_ref.shape[2]
    halves = knots // LANES
    tables = [tables_ref[k] for k in range(tables_ref.shape[0])]

    def table(c, s, h):
        return tables[(c * 2 + s) * halves + h]

    def sample(v):
        u = v * float(knots - 1)
        lower = jnp.clip(jnp.floor(u), 0.0, float(knots - 2))
        frac = u - lower
        index = lower.astype(jnp.int32)
        lane = index % LANES
        half = index // LANES
        rows = []
        for c in range(channels):
            picked = []
            for s in range(2):
                got = jnp.take_along_axis(table(c, s, 0), lane, axis=1, mode="promise_in_bounds")
                for h in range(1, halves):
                    other = jnp.take_along_axis(table(c, s, h), lane, axis=1, mode="promise_in_bounds")
                    got = jnp.where(half == h, other, got)
                picked.append(got)
            rows.append(picked[0] * (1.0 - frac) + picked[1] * frac)
        return rows

    def step(i, carry):
        r0 = pl.multiple_of(i * ROWS_PER_STEP, ROWS_PER_STEP)
        for j in range(width // LANES):
            rs = pl.ds(r0, ROWS_PER_STEP)
            ls = pl.ds(j * LANES, LANES)
            colour = None
            transmit = None
            for d in range(values_ref.shape[0]):
                smp = sample(values_ref[d, rs, ls])
                alpha = smp[channels - 1]
                if d == 0:
                    colour = [alpha * smp[c] for c in range(channels - 1)]
                    transmit = 1.0 - alpha
                else:
                    weight = transmit * alpha
                    colour = [colour[c] + weight * smp[c] for c in range(channels - 1)]
                    transmit = transmit * (1.0 - alpha)
            for c in range(channels - 1):
                out_ref[c, rs, ls] = colour[c]
            out_ref[channels - 1, rs, ls] = 1.0 - transmit
        return carry

    lax.fori_loop(0, bricks // ROWS_PER_STEP, step, 0)


def shade_bricks(values, palette):
    depth, bricks, width = values.shape
    channels, knots = palette.shape
    tables = lookup_tables(palette)

    def kernel(values_ref, tables_ref, out_ref):
        shade_kernel(knots, values_ref, tables_ref, out_ref)

    return pl.pallas_call(
        kernel,
        out_shape=jax.ShapeDtypeStruct((channels, bricks, width), jnp.float32),
        in_specs=[
            pl.BlockSpec(memory_space=pltpu.VMEM),
            pl.BlockSpec(memory_space=pltpu.VMEM),
        ],
        out_specs=pl.BlockSpec(memory_space=pltpu.VMEM),
    )(values, tables)


def composite(layers):
    while layers.shape[1] > 1:
        near_half = layers[:, 0::2]
        far_half = layers[:, 1::2]
        layers = near_half + (1.0 - near_half[3:4]) * far_half
    return layers[:, 0]


def body(bricks, colour_table, opacity_table, depth_order):
    palette = jnp.concatenate([colour_table, opacity_table[None, :]], axis=0)
    groups = lax.axis_size("grp")
    members = lax.axis_size("tile")
    devices = groups * members
    depth = bricks.shape[0]
    pixels = bricks.shape[1] * bricks.shape[2]
    block = pixels // devices
    local = bricks.reshape(depth, devices, block)
    gathered = lax.all_to_all(local, ("grp", "tile"), 1, 1, tiled=True)
    partials = shade_bricks(gathered, palette)
    by_rank = jnp.argsort(depth_order, axis=1).astype(jnp.int32)
    sequence = (jnp.arange(groups, dtype=jnp.int32)[:, None] * members + by_rank).reshape(-1)
    ordered = jnp.take(partials, sequence, axis=1)
    return composite(ordered)


def solution(mesh):
    in_specs = (P(("grp", "tile"), None, None), P(), P(), P())
    out_specs = P(None, ("grp", "tile"))
    return jax.shard_map(body, mesh=mesh, in_specs=in_specs, out_specs=out_specs, check_vma=False)
```

```python
import jax
import jax.numpy as jnp
from jax import lax
from jax.experimental import pallas as pl
from jax.experimental.pallas import tpu as pltpu
from jax.sharding import PartitionSpec as P

LANES = 128
ROWS_PER_STEP = 8


def lookup_tables(palette):
    channels, knots = palette.shape
    extended = jnp.concatenate([palette, palette[:, -1:]], axis=1)
    halves = knots // LANES
    lower = extended[:, 0:knots].reshape(channels, halves, LANES)
    upper = extended[:, 1 : knots + 1].reshape(channels, halves, LANES)
    tables = jnp.stack([lower, upper], axis=1)
    tables = jnp.broadcast_to(tables[..., None, :], (channels, 2, halves, ROWS_PER_STEP, LANES))
    return tables.reshape(channels * 2 * halves, ROWS_PER_STEP, LANES)


def shade_kernel(knots, values_ref, tables_ref, out_ref):
    channels = out_ref.shape[0]
    bricks = values_ref.shape[1]
    width = values_ref.shape[2]
    halves = knots // LANES
    tables = [tables_ref[k] for k in range(tables_ref.shape[0])]

    def table(c, s, h):
        return tables[(c * 2 + s) * halves + h]

    def sample(v):
        u = v * float(knots - 1)
        lower = jnp.clip(jnp.floor(u), 0.0, float(knots - 2))
        frac = u - lower
        index = lower.astype(jnp.int32)
        lane = index % LANES
        half = index // LANES
        rows = []
        for c in range(channels):
            picked = []
            for s in range(2):
                got = jnp.take_along_axis(table(c, s, 0), lane, axis=1, mode="promise_in_bounds")
                for h in range(1, halves):
                    other = jnp.take_along_axis(table(c, s, h), lane, axis=1, mode="promise_in_bounds")
                    got = jnp.where(half == h, other, got)
                picked.append(got)
            rows.append(picked[0] * (1.0 - frac) + picked[1] * frac)
        return rows

    def step(i, carry):
        r0 = pl.multiple_of(i * ROWS_PER_STEP, ROWS_PER_STEP)
        for j in range(width // LANES):
            rs = pl.ds(r0, ROWS_PER_STEP)
            ls = pl.ds(j * LANES, LANES)
            colour = None
            transmit = None
            for d in range(values_ref.shape[0]):
                smp = sample(values_ref[d, rs, ls])
                alpha = smp[channels - 1]
                if d == 0:
                    colour = [alpha * smp[c] for c in range(channels - 1)]
                    transmit = 1.0 - alpha
                else:
                    weight = transmit * alpha
                    colour = [colour[c] + weight * smp[c] for c in range(channels - 1)]
                    transmit = transmit * (1.0 - alpha)
            for c in range(channels - 1):
                out_ref[c, rs, ls] = colour[c]
            out_ref[channels - 1, rs, ls] = 1.0 - transmit
        return carry

    lax.fori_loop(0, bricks // ROWS_PER_STEP, step, 0)


def shade_bricks(values, palette):
    depth, bricks, width = values.shape
    channels, knots = palette.shape
    tables = lookup_tables(palette)

    def kernel(values_ref, tables_ref, out_ref):
        shade_kernel(knots, values_ref, tables_ref, out_ref)

    return pl.pallas_call(
        kernel,
        out_shape=jax.ShapeDtypeStruct((channels, bricks, width), jnp.float32),
        in_specs=[
            pl.BlockSpec(memory_space=pltpu.VMEM),
            pl.BlockSpec(memory_space=pltpu.VMEM),
        ],
        out_specs=pl.BlockSpec(memory_space=pltpu.VMEM),
    )(values, tables)


def composite(layers):
    while layers.shape[1] > 1:
        near_half = layers[:, 0::2]
        far_half = layers[:, 1::2]
        layers = near_half + (1.0 - near_half[3:4]) * far_half
    return layers[:, 0]


def exchange_kernel(send_ref, out_ref, landed, send_sem, recv_sem, own_sem):
    devices = send_ref.shape[0]
    members = lax.axis_size("tile")
    me = lax.axis_index("grp") * members + lax.axis_index("tile")

    def send(k, carry):
        dest = lax.rem(me + k, devices)
        pltpu.make_async_remote_copy(
            src_ref=send_ref.at[pl.ds(dest, 1)],
            dst_ref=landed.at[pl.ds(me, 1)],
            send_sem=send_sem,
            recv_sem=recv_sem,
            device_id=(dest // members, dest % members),
            device_id_type=pl.DeviceIdType.MESH,
        ).start()
        return carry

    lax.fori_loop(1, devices, send, 0)
    own = pltpu.make_async_copy(send_ref.at[pl.ds(me, 1)], landed.at[pl.ds(me, 1)], own_sem)
    own.start()
    own.wait()
    everything = pltpu.make_async_remote_copy(
        src_ref=send_ref.at[pl.ds(0, devices - 1)],
        dst_ref=landed.at[pl.ds(0, devices - 1)],
        send_sem=send_sem,
        recv_sem=recv_sem,
        device_id=(me // members, me % members),
        device_id_type=pl.DeviceIdType.MESH,
    )
    everything.wait_send()
    everything.wait_recv()
    out_ref[...] = landed[...]


def exchange(rows):
    return pl.pallas_call(
        exchange_kernel,
        out_shape=jax.ShapeDtypeStruct(rows.shape, rows.dtype),
        in_specs=[pl.BlockSpec(memory_space=pltpu.VMEM)],
        out_specs=pl.BlockSpec(memory_space=pltpu.VMEM),
        scratch_shapes=[
            pltpu.VMEM(rows.shape, rows.dtype),
            pltpu.SemaphoreType.DMA,
            pltpu.SemaphoreType.DMA,
            pltpu.SemaphoreType.DMA,
        ],
        compiler_params=pltpu.CompilerParams(has_side_effects=True),
    )(rows)


def body(bricks, colour_table, opacity_table, depth_order):
    palette = jnp.concatenate([colour_table, opacity_table[None, :]], axis=0)
    groups = lax.axis_size("grp")
    members = lax.axis_size("tile")
    devices = groups * members
    depth = bricks.shape[0]
    pixels = bricks.shape[1] * bricks.shape[2]
    block = pixels // devices
    rows = jnp.transpose(bricks.reshape(depth, devices, block), (1, 0, 2))
    rows = rows.reshape(devices, depth * block // LANES, LANES)
    arrived = exchange(rows)
    gathered = jnp.transpose(arrived.reshape(devices, depth, block), (1, 0, 2))
    partials = shade_bricks(gathered, palette)
    by_rank = jnp.argsort(depth_order, axis=1).astype(jnp.int32)
    sequence = (jnp.arange(groups, dtype=jnp.int32)[:, None] * members + by_rank).reshape(-1)
    ordered = jnp.take(partials, sequence, axis=1)
    return composite(ordered)


def solution(mesh):
    in_specs = (P(("grp", "tile"), None, None), P(), P(), P())
    out_specs = P(None, ("grp", "tile"))
    return jax.shard_map(body, mesh=mesh, in_specs=in_specs, out_specs=out_specs, check_vma=False)
```

```python
import functools

import jax
import jax.numpy as jnp
from jax import lax
from jax.experimental import pallas as pl
from jax.experimental.pallas import tpu as pltpu
from jax.sharding import PartitionSpec as P

LANES = 128


def render_kernel(members, values_ref, colour_ref, opacity_ref, order_ref, out_ref, parts_ref):
    tiles, sub, lanes = values_ref.shape
    knots = colour_ref.shape[1]
    halves = knots // lanes
    colours = colour_ref.shape[0]
    groups = parts_ref.shape[1] // members
    rows = [colour_ref[c : c + 1, :] for c in range(colours)] + [opacity_ref[...]]
    tables = [
        [jnp.broadcast_to(r[:, h * lanes : (h + 1) * lanes], (sub, lanes)) for h in range(halves)]
        for r in rows
    ]

    def pick(c, index):
        lane = index % lanes
        half = index // lanes
        got = jnp.take_along_axis(tables[c][0], lane, axis=1, mode="promise_in_bounds")
        for h in range(1, halves):
            other = jnp.take_along_axis(tables[c][h], lane, axis=1, mode="promise_in_bounds")
            got = jnp.where(half == h, other, got)
        return got

    def sample(v):
        u = v * float(knots - 1)
        lower = jnp.clip(jnp.floor(u), 0.0, float(knots - 2))
        frac = u - lower
        index = lower.astype(jnp.int32)
        return [pick(c, index) * (1.0 - frac) + pick(c, index + 1) * frac for c in range(colours + 1)]

    def shade(m, carry):
        front = sample(values_ref[m])
        back = [pltpu.roll(x, sub - 2, 0) for x in front]
        a0 = front[colours]
        a1 = back[colours]
        colour = [a0 * front[c] for c in range(colours)]
        transmit = 1.0 - a0
        weight = transmit * a1
        colour = [colour[c] + weight * back[c] for c in range(colours)]
        transmit = transmit * (1.0 - a1)
        part = colour + [1.0 - transmit]
        for e in range(2):
            brick = 2 * m + e
            place = (brick // members) * members + order_ref[brick]
            for c in range(colours + 1):
                parts_ref[c, place] = part[c][4 * e : 4 * e + 2]
        return carry

    lax.fori_loop(0, tiles, shade, 0)

    def blend(k, pics):
        out = []
        for g in range(groups):
            pic = pics[g]
            clear = 1.0 - pic[colours]
            out.append(tuple(pic[c] + clear * parts_ref[c, g * members + k] for c in range(colours + 1)))
        return tuple(out)

    zero = jnp.zeros((2, lanes), jnp.float32)
    pics = lax.fori_loop(0, members, blend, tuple(tuple(zero for _ in range(colours + 1)) for _ in range(groups)))
    final = pics[0]
    for g in range(1, groups):
        clear = 1.0 - final[colours]
        final = tuple(final[c] + clear * pics[g][c] for c in range(colours + 1))
    for c in range(colours + 1):
        out_ref[c] = final[c]


def render(arrived, colour_table, opacity_table, depth_order):
    devices = arrived.shape[0]
    groups, members = depth_order.shape
    lanes = arrived.shape[2]
    tiles = arrived.reshape(devices // 2, 2 * arrived.shape[1], lanes)
    channels = colour_table.shape[0] + 1
    vmem = pl.BlockSpec(memory_space=pltpu.VMEM)
    picture = pl.pallas_call(
        functools.partial(render_kernel, members),
        out_shape=jax.ShapeDtypeStruct((channels, 2, lanes), jnp.float32),
        in_specs=[vmem, vmem, vmem, pl.BlockSpec(memory_space=pltpu.SMEM)],
        out_specs=vmem,
        scratch_shapes=[pltpu.VMEM((channels, devices, 2, lanes), jnp.float32)],
    )(tiles, colour_table, opacity_table.reshape(1, -1), depth_order.reshape(-1))
    return picture.reshape(channels, 2 * lanes)


def exchange_kernel(send_ref, out_ref, landed, send_sem, recv_sem, own_sem):
    devices = send_ref.shape[0]
    members = lax.axis_size("tile")
    me = lax.axis_index("grp") * members + lax.axis_index("tile")

    def send(k, carry):
        dest = lax.rem(me + k, devices)
        pltpu.make_async_remote_copy(
            src_ref=send_ref.at[pl.ds(dest, 1)],
            dst_ref=landed.at[pl.ds(me, 1)],
            send_sem=send_sem,
            recv_sem=recv_sem,
            device_id=(dest // members, dest % members),
            device_id_type=pl.DeviceIdType.MESH,
        ).start()
        return carry

    lax.fori_loop(1, devices, send, 0)
    own = pltpu.make_async_copy(send_ref.at[pl.ds(me, 1)], landed.at[pl.ds(me, 1)], own_sem)
    own.start()
    own.wait()
    everything = pltpu.make_async_remote_copy(
        src_ref=send_ref.at[pl.ds(0, devices - 1)],
        dst_ref=landed.at[pl.ds(0, devices - 1)],
        send_sem=send_sem,
        recv_sem=recv_sem,
        device_id=(me // members, me % members),
        device_id_type=pl.DeviceIdType.MESH,
    )
    everything.wait_send()
    everything.wait_recv()
    out_ref[...] = landed[...]


def exchange(rows):
    return pl.pallas_call(
        exchange_kernel,
        out_shape=jax.ShapeDtypeStruct(rows.shape, rows.dtype),
        in_specs=[pl.BlockSpec(memory_space=pltpu.VMEM)],
        out_specs=pl.BlockSpec(memory_space=pltpu.VMEM),
        scratch_shapes=[
            pltpu.VMEM(rows.shape, rows.dtype),
            pltpu.SemaphoreType.DMA,
            pltpu.SemaphoreType.DMA,
            pltpu.SemaphoreType.DMA,
        ],
        compiler_params=pltpu.CompilerParams(has_side_effects=True),
    )(rows)


def body(bricks, colour_table, opacity_table, depth_order):
    groups = lax.axis_size("grp")
    members = lax.axis_size("tile")
    devices = groups * members
    depth = bricks.shape[0]
    pixels = bricks.shape[1] * bricks.shape[2]
    block = pixels // devices
    rows = jnp.transpose(bricks.reshape(depth, devices, block), (1, 0, 2))
    rows = rows.reshape(devices, depth * block // LANES, LANES)
    arrived = exchange(rows)
    return render(arrived, colour_table, opacity_table, depth_order)


def solution(mesh):
    in_specs = (P(("grp", "tile"), None, None), P(), P(), P())
    out_specs = P(None, ("grp", "tile"))
    return jax.shard_map(body, mesh=mesh, in_specs=in_specs, out_specs=out_specs, check_vma=False)
```

```python
import functools

import jax
import jax.numpy as jnp
from jax import lax
from jax.experimental import pallas as pl
from jax.experimental.pallas import tpu as pltpu
from jax.sharding import PartitionSpec as P

LANES = 128


def render_kernel(members, values_ref, colour_ref, opacity_ref, order_ref, out_ref, parts_ref):
    tiles, sub, lanes = values_ref.shape
    knots = colour_ref.shape[1]
    halves = knots // lanes
    colours = colour_ref.shape[0]
    groups = parts_ref.shape[1] // members
    rows = [colour_ref[c : c + 1, :] for c in range(colours)] + [opacity_ref[...]]
    tables = [
        [jnp.broadcast_to(r[:, h * lanes : (h + 1) * lanes], (sub, lanes)) for h in range(halves)]
        for r in rows
    ]

    def pick(c, index):
        lane = index % lanes
        half = index // lanes
        got = jnp.take_along_axis(tables[c][0], lane, axis=1, mode="promise_in_bounds")
        for h in range(1, halves):
            other = jnp.take_along_axis(tables[c][h], lane, axis=1, mode="promise_in_bounds")
            got = jnp.where(half == h, other, got)
        return got

    def sample(v):
        u = v * float(knots - 1)
        lower = jnp.clip(jnp.floor(u), 0.0, float(knots - 2))
        frac = u - lower
        index = lower.astype(jnp.int32)
        return [pick(c, index) * (1.0 - frac) + pick(c, index + 1) * frac for c in range(colours + 1)]

    def shade(m, carry):
        front = sample(values_ref[m])
        back = [pltpu.roll(x, sub - 2, 0) for x in front]
        a0 = front[colours]
        a1 = back[colours]
        colour = [a0 * front[c] for c in range(colours)]
        transmit = 1.0 - a0
        weight = transmit * a1
        colour = [colour[c] + weight * back[c] for c in range(colours)]
        transmit = transmit * (1.0 - a1)
        part = colour + [1.0 - transmit]
        for e in range(2):
            brick = 2 * m + e
            place = (brick // members) * members + order_ref[brick // members, brick % members]
            for c in range(colours + 1):
                parts_ref[c, place] = part[c] if e == 0 else pltpu.roll(part[c], sub - 4, 0)
        return carry

    lax.fori_loop(0, tiles, shade, 0, unroll=2)

    def blend(k, pics):
        out = []
        for g in range(groups):
            pic = pics[g]
            clear = 1.0 - pic[colours]
            out.append(tuple(pic[c] + clear * parts_ref[c, g * members + k] for c in range(colours + 1)))
        return tuple(out)

    zero = jnp.zeros((sub, lanes), jnp.float32)
    start = tuple(tuple(zero for _ in range(colours + 1)) for _ in range(groups))
    pics = lax.fori_loop(0, members, blend, start, unroll=4)
    final = pics[0]
    for g in range(1, groups):
        clear = 1.0 - final[colours]
        final = tuple(final[c] + clear * pics[g][c] for c in range(colours + 1))
    for c in range(colours + 1):
        for j in range(2):
            out_ref[c : c + 1, j * lanes : (j + 1) * lanes] = final[c][j : j + 1]


def render(arrived, colour_table, opacity_table, depth_order):
    devices = arrived.shape[0]
    groups, members = depth_order.shape
    lanes = arrived.shape[2]
    sub = 2 * arrived.shape[1]
    tiles = arrived.reshape(devices // 2, sub, lanes)
    channels = colour_table.shape[0] + 1
    vmem = pl.BlockSpec(memory_space=pltpu.VMEM)
    return pl.pallas_call(
        functools.partial(render_kernel, members),
        out_shape=jax.ShapeDtypeStruct((channels, 2 * lanes), jnp.float32),
        in_specs=[vmem, vmem, vmem, pl.BlockSpec(memory_space=pltpu.SMEM)],
        out_specs=vmem,
        scratch_shapes=[pltpu.VMEM((channels, devices, sub, lanes), jnp.float32)],
    )(tiles, colour_table, opacity_table.reshape(1, -1), depth_order)


def exchange_kernel(send_ref, out_ref, landed, send_sem, recv_sem, own_sem):
    devices = send_ref.shape[0]
    members = lax.axis_size("tile")
    me = lax.axis_index("grp") * members + lax.axis_index("tile")

    def send(k, carry):
        dest = lax.rem(me + k, devices)
        pltpu.make_async_remote_copy(
            src_ref=send_ref.at[pl.ds(dest, 1)],
            dst_ref=landed.at[pl.ds(me, 1)],
            send_sem=send_sem,
            recv_sem=recv_sem,
            device_id=(dest // members, dest % members),
            device_id_type=pl.DeviceIdType.MESH,
        ).start()
        return carry

    lax.fori_loop(1, devices, send, 0)
    own = pltpu.make_async_copy(send_ref.at[pl.ds(me, 1)], landed.at[pl.ds(me, 1)], own_sem)
    own.start()
    own.wait()
    everything = pltpu.make_async_remote_copy(
        src_ref=send_ref.at[pl.ds(0, devices - 1)],
        dst_ref=landed.at[pl.ds(0, devices - 1)],
        send_sem=send_sem,
        recv_sem=recv_sem,
        device_id=(me // members, me % members),
        device_id_type=pl.DeviceIdType.MESH,
    )
    everything.wait_send()
    everything.wait_recv()
    out_ref[...] = landed[...]


def exchange(rows):
    return pl.pallas_call(
        exchange_kernel,
        out_shape=jax.ShapeDtypeStruct(rows.shape, rows.dtype),
        in_specs=[pl.BlockSpec(memory_space=pltpu.VMEM)],
        out_specs=pl.BlockSpec(memory_space=pltpu.VMEM),
        scratch_shapes=[
            pltpu.VMEM(rows.shape, rows.dtype),
            pltpu.SemaphoreType.DMA,
            pltpu.SemaphoreType.DMA,
            pltpu.SemaphoreType.DMA,
        ],
        compiler_params=pltpu.CompilerParams(has_side_effects=True),
    )(rows)


def body(bricks, colour_table, opacity_table, depth_order):
    groups = lax.axis_size("grp")
    members = lax.axis_size("tile")
    devices = groups * members
    depth = bricks.shape[0]
    pixels = bricks.shape[1] * bricks.shape[2]
    block = pixels // devices
    rows = jnp.transpose(bricks.reshape(depth, devices, block), (1, 0, 2))
    rows = rows.reshape(devices, depth * block // LANES, LANES)
    arrived = exchange(rows)
    return render(arrived, colour_table, opacity_table, depth_order)


def solution(mesh):
    in_specs = (P(("grp", "tile"), None, None), P(), P(), P())
    out_specs = P(None, ("grp", "tile"))
    return jax.shard_map(body, mesh=mesh, in_specs=in_specs, out_specs=out_specs, check_vma=False)
```

```python
import functools
import math

import jax
import jax.numpy as jnp
from jax import lax
from jax.experimental import pallas as pl
from jax.experimental.pallas import tpu as pltpu
from jax.sharding import PartitionSpec as P

LANES = 128


def render_kernel(members, values_ref, colour_ref, opacity_ref, order_ref, out_ref, parts_ref):
    tiles, sub, lanes = values_ref.shape
    knots = colour_ref.shape[1]
    halves = knots // lanes
    colours = colour_ref.shape[0]
    groups = parts_ref.shape[1] // members
    rows = [colour_ref[c : c + 1, :] for c in range(colours)] + [opacity_ref[...]]
    tables = [
        [jnp.broadcast_to(r[:, h * lanes : (h + 1) * lanes], (sub, lanes)) for h in range(halves)]
        for r in rows
    ]

    def pick(c, index):
        lane = index % lanes
        half = index // lanes
        got = jnp.take_along_axis(tables[c][0], lane, axis=1, mode="promise_in_bounds")
        for h in range(1, halves):
            other = jnp.take_along_axis(tables[c][h], lane, axis=1, mode="promise_in_bounds")
            got = jnp.where(half == h, other, got)
        return got

    def sample(v):
        u = v * float(knots - 1)
        lower = jnp.clip(jnp.floor(u), 0.0, float(knots - 2))
        frac = u - lower
        index = lower.astype(jnp.int32)
        return [pick(c, index) * (1.0 - frac) + pick(c, index + 1) * frac for c in range(colours + 1)]

    def shade(m, carry):
        front = sample(values_ref[m])
        back = [pltpu.roll(x, sub - 2, 0) for x in front]
        a0 = front[colours]
        a1 = back[colours]
        colour = [a0 * front[c] for c in range(colours)]
        transmit = 1.0 - a0
        weight = transmit * a1
        colour = [colour[c] + weight * back[c] for c in range(colours)]
        transmit = transmit * (1.0 - a1)
        part = colour + [1.0 - transmit]
        for e in range(2):
            brick = 2 * m + e
            place = (brick // members) * members + order_ref[brick // members, brick % members]
            for c in range(colours + 1):
                parts_ref[c, place] = part[c] if e == 0 else pltpu.roll(part[c], sub - 4, 0)
        return carry

    lax.fori_loop(0, tiles, shade, 0, unroll=2)

    def blend(k, pics):
        out = []
        for g in range(groups):
            pic = pics[g]
            clear = 1.0 - pic[colours]
            out.append(tuple(pic[c] + clear * parts_ref[c, g * members + k] for c in range(colours + 1)))
        return tuple(out)

    zero = jnp.zeros((sub, lanes), jnp.float32)
    start = tuple(tuple(zero for _ in range(colours + 1)) for _ in range(groups))
    pics = lax.fori_loop(0, members, blend, start, unroll=4)
    final = pics[0]
    for g in range(1, groups):
        clear = 1.0 - final[colours]
        final = tuple(final[c] + clear * pics[g][c] for c in range(colours + 1))
    for c in range(colours + 1):
        for j in range(2):
            out_ref[c : c + 1, j * lanes : (j + 1) * lanes] = final[c][j : j + 1]


def render(arrived, colour_table, opacity_table, depth_order):
    devices = arrived.shape[0]
    groups, members = depth_order.shape
    lanes = arrived.shape[2]
    sub = 2 * arrived.shape[1]
    tiles = arrived.reshape(devices // 2, sub, lanes)
    channels = colour_table.shape[0] + 1
    vmem = pl.BlockSpec(memory_space=pltpu.VMEM)
    return pl.pallas_call(
        functools.partial(render_kernel, members),
        out_shape=jax.ShapeDtypeStruct((channels, 2 * lanes), jnp.float32),
        in_specs=[vmem, vmem, vmem, pl.BlockSpec(memory_space=pltpu.SMEM)],
        out_specs=vmem,
        scratch_shapes=[pltpu.VMEM((channels, devices, sub, lanes), jnp.float32)],
    )(tiles, colour_table, opacity_table.reshape(1, -1), depth_order)


def spread_stride(devices):
    step = (3 * devices) // 8 + 1
    while math.gcd(step, devices) != 1:
        step += 1
    return step


def exchange_kernel(send_ref, out_ref, landed, send_sem, recv_sem, own_sem):
    devices = send_ref.shape[0]
    members = lax.axis_size("tile")
    me = lax.axis_index("grp") * members + lax.axis_index("tile")

    stride = spread_stride(devices)

    def send(k, carry):
        dest = lax.rem(me + k * stride, devices)
        pltpu.make_async_remote_copy(
            src_ref=send_ref.at[pl.ds(dest, 1)],
            dst_ref=landed.at[pl.ds(me, 1)],
            send_sem=send_sem,
            recv_sem=recv_sem,
            device_id=(dest // members, dest % members),
            device_id_type=pl.DeviceIdType.MESH,
        ).start()
        return carry

    lax.fori_loop(1, devices, send, 0)
    own = pltpu.make_async_copy(send_ref.at[pl.ds(me, 1)], landed.at[pl.ds(me, 1)], own_sem)
    own.start()
    own.wait()
    everything = pltpu.make_async_remote_copy(
        src_ref=send_ref.at[pl.ds(0, devices - 1)],
        dst_ref=landed.at[pl.ds(0, devices - 1)],
        send_sem=send_sem,
        recv_sem=recv_sem,
        device_id=(me // members, me % members),
        device_id_type=pl.DeviceIdType.MESH,
    )
    everything.wait_send()
    everything.wait_recv()
    out_ref[...] = landed[...]


def exchange(rows):
    return pl.pallas_call(
        exchange_kernel,
        out_shape=jax.ShapeDtypeStruct(rows.shape, rows.dtype),
        in_specs=[pl.BlockSpec(memory_space=pltpu.VMEM)],
        out_specs=pl.BlockSpec(memory_space=pltpu.VMEM),
        scratch_shapes=[
            pltpu.VMEM(rows.shape, rows.dtype),
            pltpu.SemaphoreType.DMA,
            pltpu.SemaphoreType.DMA,
            pltpu.SemaphoreType.DMA,
        ],
        compiler_params=pltpu.CompilerParams(has_side_effects=True),
    )(rows)


def body(bricks, colour_table, opacity_table, depth_order):
    groups = lax.axis_size("grp")
    members = lax.axis_size("tile")
    devices = groups * members
    depth = bricks.shape[0]
    pixels = bricks.shape[1] * bricks.shape[2]
    block = pixels // devices
    rows = jnp.transpose(bricks.reshape(depth, devices, block), (1, 0, 2))
    rows = rows.reshape(devices, depth * block // LANES, LANES)
    arrived = exchange(rows)
    return render(arrived, colour_table, opacity_table, depth_order)


def solution(mesh):
    in_specs = (P(("grp", "tile"), None, None), P(), P(), P())
    out_specs = P(None, ("grp", "tile"))
    return jax.shard_map(body, mesh=mesh, in_specs=in_specs, out_specs=out_specs, check_vma=False)
```

```python
import functools

import jax
import jax.numpy as jnp
from jax import lax
from jax.experimental import pallas as pl
from jax.experimental.pallas import tpu as pltpu
from jax.sharding import PartitionSpec as P

LANES = 128


def make_sampler(colour_ref, opacity_ref, sub):
    knots = colour_ref.shape[1]
    lanes = LANES
    halves = knots // lanes
    colours = colour_ref.shape[0]
    rows = [colour_ref[c : c + 1, :] for c in range(colours)] + [opacity_ref[...]]
    tables = [
        [jnp.broadcast_to(r[:, h * lanes : (h + 1) * lanes], (sub, lanes)) for h in range(halves)]
        for r in rows
    ]

    def pick(c, index):
        lane = index % lanes
        half = index // lanes
        got = jnp.take_along_axis(tables[c][0], lane, axis=1, mode="promise_in_bounds")
        for h in range(1, halves):
            other = jnp.take_along_axis(tables[c][h], lane, axis=1, mode="promise_in_bounds")
            got = jnp.where(half == h, other, got)
        return got

    def sample(v):
        u = v * float(knots - 1)
        lower = jnp.clip(jnp.floor(u), 0.0, float(knots - 2))
        frac = u - lower
        index = lower.astype(jnp.int32)
        return [pick(c, index) * (1.0 - frac) + pick(c, index + 1) * frac for c in range(colours + 1)]

    return sample


def shade_tile(sample, v):
    sub = v.shape[0]
    front = sample(v)
    colours = len(front) - 1
    back = [pltpu.roll(x, sub - 2, 0) for x in front]
    a0 = front[colours]
    a1 = back[colours]
    colour = [a0 * front[c] for c in range(colours)]
    transmit = 1.0 - a0
    weight = transmit * a1
    colour = [colour[c] + weight * back[c] for c in range(colours)]
    transmit = transmit * (1.0 - a1)
    return colour + [1.0 - transmit]


def composite_kernel(members, partial_ref, order_ref, out_ref, parts_ref):
    channels, tiles, sub, lanes = partial_ref.shape
    colours = channels - 1
    groups = parts_ref.shape[1] // members

    def scatter(m, carry):
        for e in range(2):
            brick = 2 * m + e
            place = (brick // members) * members + order_ref[brick // members, brick % members]
            for c in range(channels):
                part = partial_ref[c, m]
                parts_ref[c, place] = part if e == 0 else pltpu.roll(part, sub - 4, 0)
        return carry

    lax.fori_loop(0, tiles, scatter, 0, unroll=2)

    def blend(k, pics):
        out = []
        for g in range(groups):
            pic = pics[g]
            clear = 1.0 - pic[colours]
            out.append(tuple(pic[c] + clear * parts_ref[c, g * members + k] for c in range(channels)))
        return tuple(out)

    zero = jnp.zeros((sub, lanes), jnp.float32)
    start = tuple(tuple(zero for _ in range(channels)) for _ in range(groups))
    pics = lax.fori_loop(0, members, blend, start, unroll=4)
    final = pics[0]
    for g in range(1, groups):
        clear = 1.0 - final[colours]
        final = tuple(final[c] + clear * pics[g][c] for c in range(channels))
    for c in range(channels):
        for j in range(2):
            out_ref[c : c + 1, j * lanes : (j + 1) * lanes] = final[c][j : j + 1]


def composite(partials, depth_order):
    channels, tiles, sub, lanes = partials.shape
    groups, members = depth_order.shape
    vmem = pl.BlockSpec(memory_space=pltpu.VMEM)
    return pl.pallas_call(
        functools.partial(composite_kernel, members),
        out_shape=jax.ShapeDtypeStruct((channels, 2 * lanes), jnp.float32),
        in_specs=[vmem, pl.BlockSpec(memory_space=pltpu.SMEM)],
        out_specs=vmem,
        scratch_shapes=[pltpu.VMEM((channels, 2 * tiles, sub, lanes), jnp.float32)],
    )(partials, depth_order)


def exchange_kernel(send_ref, colour_ref, opacity_ref, out_ref, landed, send_sem, recv_sem):
    devices = send_ref.shape[0]
    rows = send_ref.shape[1]
    members = lax.axis_size("tile")
    me = lax.axis_index("grp") * members + lax.axis_index("tile")

    def copy_to(dest, source):
        return pltpu.make_async_remote_copy(
            src_ref=send_ref.at[pl.ds(dest, 1)],
            dst_ref=landed.at[pl.ds(source, 1)],
            send_sem=send_sem,
            recv_sem=recv_sem.at[source],
            device_id=(dest // members, dest % members),
            device_id_type=pl.DeviceIdType.MESH,
        )

    def send(k, carry):
        copy_to(lax.rem(me + k, devices), me).start()
        return carry

    lax.fori_loop(1, devices, send, 0)
    landed[pl.ds(me, 1)] = send_ref[pl.ds(me, 1)]
    sample = make_sampler(colour_ref, opacity_ref, 2 * rows)
    tiles = devices // 2
    first = me // 2

    def shade(i, carry):
        m = lax.rem(first - i + tiles, tiles)
        for e in range(2):
            source = 2 * m + e

            @pl.when(source != me)
            def _():
                copy_to(me, source).wait_recv()

        v = jnp.concatenate([landed[2 * m], landed[2 * m + 1]], axis=0)
        part = shade_tile(sample, v)
        for c in range(len(part)):
            out_ref[c, m] = part[c]
        return carry

    lax.fori_loop(0, tiles, shade, 0)
    everything = pltpu.make_async_remote_copy(
        src_ref=send_ref.at[pl.ds(0, devices - 1)],
        dst_ref=landed.at[pl.ds(0, devices - 1)],
        send_sem=send_sem,
        recv_sem=recv_sem.at[me],
        device_id=(me // members, me % members),
        device_id_type=pl.DeviceIdType.MESH,
    )
    everything.wait_send()


def exchange_and_shade(rows, colour_table, opacity_table):
    devices, sub, lanes = rows.shape
    channels = colour_table.shape[0] + 1
    vmem = pl.BlockSpec(memory_space=pltpu.VMEM)
    return pl.pallas_call(
        exchange_kernel,
        out_shape=jax.ShapeDtypeStruct((channels, devices // 2, 2 * sub, lanes), jnp.float32),
        in_specs=[vmem, vmem, vmem],
        out_specs=vmem,
        scratch_shapes=[
            pltpu.VMEM(rows.shape, rows.dtype),
            pltpu.SemaphoreType.DMA,
            pltpu.SemaphoreType.DMA((devices,)),
        ],
        compiler_params=pltpu.CompilerParams(has_side_effects=True),
    )(rows, colour_table, opacity_table.reshape(1, -1))


def body(bricks, colour_table, opacity_table, depth_order):
    groups = lax.axis_size("grp")
    members = lax.axis_size("tile")
    devices = groups * members
    depth = bricks.shape[0]
    pixels = bricks.shape[1] * bricks.shape[2]
    block = pixels // devices
    rows = jnp.transpose(bricks.reshape(depth, devices, block), (1, 0, 2))
    rows = rows.reshape(devices, depth * block // LANES, LANES)
    partials = exchange_and_shade(rows, colour_table, opacity_table)
    return composite(partials, depth_order)


def solution(mesh):
    in_specs = (P(("grp", "tile"), None, None), P(), P(), P())
    out_specs = P(None, ("grp", "tile"))
    return jax.shard_map(body, mesh=mesh, in_specs=in_specs, out_specs=out_specs, check_vma=False)
```

```python
import functools

import jax
import jax.numpy as jnp
from jax import lax
from jax.experimental import pallas as pl
from jax.experimental.pallas import tpu as pltpu
from jax.sharding import PartitionSpec as P

LANES = 128


def render_kernel(members, values_ref, colour_ref, opacity_ref, order_ref, out_ref, parts_ref):
    tiles, sub, lanes = values_ref.shape
    knots = colour_ref.shape[1]
    halves = knots // lanes
    colours = colour_ref.shape[0]
    groups = parts_ref.shape[1] // members
    rows = [colour_ref[c : c + 1, :] for c in range(colours)] + [opacity_ref[...]]
    tables = [
        [jnp.broadcast_to(r[:, h * lanes : (h + 1) * lanes], (sub, lanes)) for h in range(halves)]
        for r in rows
    ]

    def pick(c, index):
        lane = index % lanes
        half = index // lanes
        got = jnp.take_along_axis(tables[c][0], lane, axis=1, mode="promise_in_bounds")
        for h in range(1, halves):
            other = jnp.take_along_axis(tables[c][h], lane, axis=1, mode="promise_in_bounds")
            got = jnp.where(half == h, other, got)
        return got

    def sample(v):
        u = v * float(knots - 1)
        lower = jnp.clip(jnp.floor(u), 0.0, float(knots - 2))
        frac = u - lower
        index = lower.astype(jnp.int32)
        return [pick(c, index) * (1.0 - frac) + pick(c, index + 1) * frac for c in range(colours + 1)]

    def shade(m, carry):
        front = sample(values_ref[m])
        back = [pltpu.roll(x, sub - 2, 0) for x in front]
        a0 = front[colours]
        a1 = back[colours]
        colour = [a0 * front[c] for c in range(colours)]
        transmit = 1.0 - a0
        weight = transmit * a1
        colour = [colour[c] + weight * back[c] for c in range(colours)]
        transmit = transmit * (1.0 - a1)
        part = colour + [1.0 - transmit]
        for e in range(2):
            brick = 2 * m + e
            place = (brick // members) * members + order_ref[brick // members, brick % members]
            for c in range(colours + 1):
                parts_ref[c, place] = part[c] if e == 0 else pltpu.roll(part[c], sub - 4, 0)
        return carry

    lax.fori_loop(0, tiles, shade, 0, unroll=2)

    def blend(k, pics):
        out = []
        for g in range(groups):
            pic = pics[g]
            clear = 1.0 - pic[colours]
            out.append(tuple(pic[c] + clear * parts_ref[c, g * members + k] for c in range(colours + 1)))
        return tuple(out)

    zero = jnp.zeros((sub, lanes), jnp.float32)
    start = tuple(tuple(zero for _ in range(colours + 1)) for _ in range(groups))
    pics = lax.fori_loop(0, members, blend, start, unroll=4)
    final = pics[0]
    for g in range(1, groups):
        clear = 1.0 - final[colours]
        final = tuple(final[c] + clear * pics[g][c] for c in range(colours + 1))
    for c in range(colours + 1):
        for j in range(2):
            out_ref[c : c + 1, j * lanes : (j + 1) * lanes] = final[c][j : j + 1]


def render(arrived, colour_table, opacity_table, depth_order):
    devices = arrived.shape[0]
    groups, members = depth_order.shape
    lanes = arrived.shape[2]
    sub = 2 * arrived.shape[1]
    tiles = arrived.reshape(devices // 2, sub, lanes)
    channels = colour_table.shape[0] + 1
    vmem = pl.BlockSpec(memory_space=pltpu.VMEM)
    return pl.pallas_call(
        functools.partial(render_kernel, members),
        out_shape=jax.ShapeDtypeStruct((channels, 2 * lanes), jnp.float32),
        in_specs=[vmem, vmem, vmem, pl.BlockSpec(memory_space=pltpu.SMEM)],
        out_specs=vmem,
        scratch_shapes=[pltpu.VMEM((channels, devices, sub, lanes), jnp.float32)],
    )(tiles, colour_table, opacity_table.reshape(1, -1), depth_order)


def exchange_kernel(send_ref, out_ref, middle, landed, sems):
    members, groups = send_ref.shape[0], send_ref.shape[1]
    g = lax.axis_index("grp")
    t = lax.axis_index("tile")
    send1, recv1, send2, recv2, own = (sems.at[i] for i in range(5))

    def first(k, carry):
        peer = lax.rem(t + k, members)
        pltpu.make_async_remote_copy(
            src_ref=send_ref.at[pl.ds(peer, 1)],
            dst_ref=middle.at[pl.ds(t, 1)],
            send_sem=send1,
            recv_sem=recv1,
            device_id=(g, peer),
            device_id_type=pl.DeviceIdType.MESH,
        ).start()
        return carry

    lax.fori_loop(1, members, first, 0)
    middle[pl.ds(t, 1)] = send_ref[pl.ds(t, 1)]
    stage1 = pltpu.make_async_remote_copy(
        src_ref=send_ref.at[pl.ds(0, members - 1)],
        dst_ref=middle.at[pl.ds(0, members - 1)],
        send_sem=send1,
        recv_sem=recv1,
        device_id=(g, t),
        device_id_type=pl.DeviceIdType.MESH,
    )
    stage1.wait_recv()

    def second(k, carry):
        peer = lax.rem(g + k, groups)
        pltpu.make_async_remote_copy(
            src_ref=middle.at[:, peer],
            dst_ref=landed.at[g],
            send_sem=send2,
            recv_sem=recv2,
            device_id=(peer, t),
            device_id_type=pl.DeviceIdType.MESH,
        ).start()
        return carry

    lax.fori_loop(1, groups, second, 0)
    mine = pltpu.make_async_copy(middle.at[:, g], landed.at[g], own)
    mine.start()
    mine.wait()
    stage2 = pltpu.make_async_remote_copy(
        src_ref=landed.at[pl.ds(0, groups - 1)],
        dst_ref=landed.at[pl.ds(0, groups - 1)],
        send_sem=send2,
        recv_sem=recv2,
        device_id=(g, t),
        device_id_type=pl.DeviceIdType.MESH,
    )
    stage2.wait_recv()
    stage1.wait_send()
    stage2.wait_send()
    out_ref[...] = landed[...]


def exchange(rows, groups):
    devices, sub, lanes = rows.shape
    members = devices // groups
    send = jnp.transpose(rows.reshape(groups, members, sub, lanes), (1, 0, 2, 3))
    arrived = pl.pallas_call(
        exchange_kernel,
        out_shape=jax.ShapeDtypeStruct((groups, members, sub, lanes), rows.dtype),
        in_specs=[pl.BlockSpec(memory_space=pltpu.VMEM)],
        out_specs=pl.BlockSpec(memory_space=pltpu.VMEM),
        scratch_shapes=[
            pltpu.VMEM((members, groups, sub, lanes), rows.dtype),
            pltpu.VMEM((groups, members, sub, lanes), rows.dtype),
            pltpu.SemaphoreType.DMA((5,)),
        ],
        compiler_params=pltpu.CompilerParams(has_side_effects=True),
    )(send)
    return arrived.reshape(devices, sub, lanes)


def body(bricks, colour_table, opacity_table, depth_order):
    groups = lax.axis_size("grp")
    members = lax.axis_size("tile")
    devices = groups * members
    depth = bricks.shape[0]
    pixels = bricks.shape[1] * bricks.shape[2]
    block = pixels // devices
    rows = jnp.transpose(bricks.reshape(depth, devices, block), (1, 0, 2))
    rows = rows.reshape(devices, depth * block // LANES, LANES)
    arrived = exchange(rows, groups)
    return render(arrived, colour_table, opacity_table, depth_order)


def solution(mesh):
    in_specs = (P(("grp", "tile"), None, None), P(), P(), P())
    out_specs = P(None, ("grp", "tile"))
    return jax.shard_map(body, mesh=mesh, in_specs=in_specs, out_specs=out_specs, check_vma=False)
```

```python
import functools

import jax
import jax.numpy as jnp
from jax import lax
from jax.experimental import pallas as pl
from jax.experimental.pallas import tpu as pltpu
from jax.sharding import PartitionSpec as P

LANES = 128


def render_kernel(members, values_ref, colour_ref, opacity_ref, order_ref, out_ref, parts_ref):
    tiles, sub, lanes = values_ref.shape
    knots = colour_ref.shape[1]
    halves = knots // lanes
    colours = colour_ref.shape[0]
    groups = parts_ref.shape[1] // members
    rows = [colour_ref[c : c + 1, :] for c in range(colours)] + [opacity_ref[...]]
    tables = [
        [jnp.broadcast_to(r[:, h * lanes : (h + 1) * lanes], (sub, lanes)) for h in range(halves)]
        for r in rows
    ]
    last_lane = lax.broadcasted_iota(jnp.int32, (sub, lanes), 1) == lanes - 1
    uppers = []
    for per_half in tables:
        shifted = [pltpu.roll(x, lanes - 1, 1) for x in per_half]
        uppers.append(
            [jnp.where(last_lane, shifted[h + 1], shifted[h]) if h + 1 < halves else shifted[h] for h in range(halves)]
        )

    def pick(table, lane, in_half):
        got = jnp.take_along_axis(table[0], lane, axis=1, mode="promise_in_bounds")
        for h in range(1, halves):
            other = jnp.take_along_axis(table[h], lane, axis=1, mode="promise_in_bounds")
            got = jnp.where(in_half[h], other, got)
        return got

    def sample(v):
        u = v * float(knots - 1)
        lower = jnp.clip(jnp.floor(u), 0.0, float(knots - 2))
        frac = u - lower
        index = lower.astype(jnp.int32)
        lane = index % lanes
        half = index // lanes
        in_half = [None] + [half == h for h in range(1, halves)]
        return [
            pick(tables[c], lane, in_half) * (1.0 - frac) + pick(uppers[c], lane, in_half) * frac
            for c in range(colours + 1)
        ]

    def shade(m, carry):
        front = sample(values_ref[m])
        back = [pltpu.roll(x, sub - 2, 0) for x in front]
        a0 = front[colours]
        a1 = back[colours]
        colour = [a0 * front[c] for c in range(colours)]
        transmit = 1.0 - a0
        weight = transmit * a1
        colour = [colour[c] + weight * back[c] for c in range(colours)]
        transmit = transmit * (1.0 - a1)
        part = colour + [1.0 - transmit]
        for e in range(2):
            brick = 2 * m + e
            place = (brick // members) * members + order_ref[brick // members, brick % members]
            for c in range(colours + 1):
                parts_ref[c, place] = part[c] if e == 0 else pltpu.roll(part[c], sub - 4, 0)
        return carry

    lax.fori_loop(0, tiles, shade, 0, unroll=4)

    def blend(k, pics):
        out = []
        for g in range(groups):
            pic = pics[g]
            clear = 1.0 - pic[colours]
            out.append(tuple(pic[c] + clear * parts_ref[c, g * members + k] for c in range(colours + 1)))
        return tuple(out)

    zero = jnp.zeros((sub, lanes), jnp.float32)
    start = tuple(tuple(zero for _ in range(colours + 1)) for _ in range(groups))
    pics = lax.fori_loop(0, members, blend, start, unroll=4)
    final = pics[0]
    for g in range(1, groups):
        clear = 1.0 - final[colours]
        final = tuple(final[c] + clear * pics[g][c] for c in range(colours + 1))
    for c in range(colours + 1):
        for j in range(2):
            out_ref[c : c + 1, j * lanes : (j + 1) * lanes] = final[c][j : j + 1]


def render(arrived, colour_table, opacity_table, depth_order):
    devices = arrived.shape[0]
    groups, members = depth_order.shape
    lanes = arrived.shape[2]
    sub = 2 * arrived.shape[1]
    tiles = arrived.reshape(devices // 2, sub, lanes)
    channels = colour_table.shape[0] + 1
    vmem = pl.BlockSpec(memory_space=pltpu.VMEM)
    return pl.pallas_call(
        functools.partial(render_kernel, members),
        out_shape=jax.ShapeDtypeStruct((channels, 2 * lanes), jnp.float32),
        in_specs=[vmem, vmem, vmem, pl.BlockSpec(memory_space=pltpu.SMEM)],
        out_specs=vmem,
        scratch_shapes=[pltpu.VMEM((channels, devices, sub, lanes), jnp.float32)],
    )(tiles, colour_table, opacity_table.reshape(1, -1), depth_order)


def exchange_kernel(send_ref, out_ref, landed, send_sem, recv_sem, own_sem):
    devices = send_ref.shape[0]
    members = lax.axis_size("tile")
    me = lax.axis_index("grp") * members + lax.axis_index("tile")

    def send(k, carry):
        dest = lax.rem(me + k, devices)
        pltpu.make_async_remote_copy(
            src_ref=send_ref.at[pl.ds(dest, 1)],
            dst_ref=landed.at[pl.ds(me, 1)],
            send_sem=send_sem,
            recv_sem=recv_sem,
            device_id=(dest // members, dest % members),
            device_id_type=pl.DeviceIdType.MESH,
        ).start()
        return carry

    lax.fori_loop(1, devices, send, 0)
    own = pltpu.make_async_copy(send_ref.at[pl.ds(me, 1)], landed.at[pl.ds(me, 1)], own_sem)
    own.start()
    own.wait()
    everything = pltpu.make_async_remote_copy(
        src_ref=send_ref.at[pl.ds(0, devices - 1)],
        dst_ref=landed.at[pl.ds(0, devices - 1)],
        send_sem=send_sem,
        recv_sem=recv_sem,
        device_id=(me // members, me % members),
        device_id_type=pl.DeviceIdType.MESH,
    )
    everything.wait_send()
    everything.wait_recv()
    out_ref[...] = landed[...]


def exchange(rows):
    return pl.pallas_call(
        exchange_kernel,
        out_shape=jax.ShapeDtypeStruct(rows.shape, rows.dtype),
        in_specs=[pl.BlockSpec(memory_space=pltpu.VMEM)],
        out_specs=pl.BlockSpec(memory_space=pltpu.VMEM),
        scratch_shapes=[
            pltpu.VMEM(rows.shape, rows.dtype),
            pltpu.SemaphoreType.DMA,
            pltpu.SemaphoreType.DMA,
            pltpu.SemaphoreType.DMA,
        ],
        compiler_params=pltpu.CompilerParams(has_side_effects=True),
    )(rows)


def body(bricks, colour_table, opacity_table, depth_order):
    groups = lax.axis_size("grp")
    members = lax.axis_size("tile")
    devices = groups * members
    depth = bricks.shape[0]
    pixels = bricks.shape[1] * bricks.shape[2]
    block = pixels // devices
    rows = jnp.transpose(bricks.reshape(depth, devices, block), (1, 0, 2))
    rows = rows.reshape(devices, depth * block // LANES, LANES)
    arrived = exchange(rows)
    return render(arrived, colour_table, opacity_table, depth_order)


def solution(mesh):
    in_specs = (P(("grp", "tile"), None, None), P(), P(), P())
    out_specs = P(None, ("grp", "tile"))
    return jax.shard_map(body, mesh=mesh, in_specs=in_specs, out_specs=out_specs, check_vma=False)
```

```python
import functools

import jax
import jax.numpy as jnp
from jax import lax
from jax.experimental import pallas as pl
from jax.experimental.pallas import tpu as pltpu
from jax.sharding import PartitionSpec as P

LANES = 128


def render_kernel(members, values_ref, colour_ref, opacity_ref, order_ref, out_ref, parts_ref):
    tiles, sub, lanes = values_ref.shape
    knots = colour_ref.shape[1]
    halves = knots // lanes
    colours = colour_ref.shape[0]
    groups = parts_ref.shape[1] // members
    rows = [colour_ref[c : c + 1, :] for c in range(colours)] + [opacity_ref[...]]
    tables = [
        [jnp.broadcast_to(r[:, h * lanes : (h + 1) * lanes], (sub, lanes)) for h in range(halves)]
        for r in rows
    ]
    last_lane = lax.broadcasted_iota(jnp.int32, (sub, lanes), 1) == lanes - 1
    uppers = []
    for per_half in tables:
        shifted = [pltpu.roll(x, lanes - 1, 1) for x in per_half]
        uppers.append(
            [jnp.where(last_lane, shifted[h + 1], shifted[h]) if h + 1 < halves else shifted[h] for h in range(halves)]
        )

    def pick(table, lane, in_half):
        got = jnp.take_along_axis(table[0], lane, axis=1, mode="promise_in_bounds")
        for h in range(1, halves):
            other = jnp.take_along_axis(table[h], lane, axis=1, mode="promise_in_bounds")
            got = jnp.where(in_half[h], other, got)
        return got

    def sample(v):
        u = v * float(knots - 1)
        lower = jnp.clip(jnp.floor(u), 0.0, float(knots - 2))
        frac = u - lower
        index = lower.astype(jnp.int32)
        lane = index % lanes
        half = index // lanes
        in_half = [None] + [half == h for h in range(1, halves)]
        return [
            pick(tables[c], lane, in_half) * (1.0 - frac) + pick(uppers[c], lane, in_half) * frac
            for c in range(colours + 1)
        ]

    def shade(m, carry):
        front = sample(values_ref[m])
        back = [pltpu.roll(x, sub - 2, 0) for x in front]
        a0 = front[colours]
        a1 = back[colours]
        colour = [a0 * front[c] for c in range(colours)]
        transmit = 1.0 - a0
        weight = transmit * a1
        colour = [colour[c] + weight * back[c] for c in range(colours)]
        transmit = transmit * (1.0 - a1)
        part = colour + [1.0 - transmit]
        for e in range(2):
            brick = 2 * m + e
            place = (brick // members) * members + order_ref[brick // members, brick % members]
            for c in range(colours + 1):
                parts_ref[c, place] = part[c] if e == 0 else pltpu.roll(part[c], sub - 4, 0)
        return carry

    lax.fori_loop(0, tiles, shade, 0, unroll=16)

    def blend(k, pics):
        out = []
        for g in range(groups):
            pic = pics[g]
            clear = 1.0 - pic[colours]
            out.append(tuple(pic[c] + clear * parts_ref[c, g * members + k] for c in range(colours + 1)))
        return tuple(out)

    zero = jnp.zeros((sub, lanes), jnp.float32)
    start = tuple(tuple(zero for _ in range(colours + 1)) for _ in range(groups))
    pics = lax.fori_loop(0, members, blend, start, unroll=4)
    final = pics[0]
    for g in range(1, groups):
        clear = 1.0 - final[colours]
        final = tuple(final[c] + clear * pics[g][c] for c in range(colours + 1))
    for c in range(colours + 1):
        for j in range(2):
            out_ref[c : c + 1, j * lanes : (j + 1) * lanes] = final[c][j : j + 1]


def render(arrived, colour_table, opacity_table, depth_order):
    devices = arrived.shape[0]
    groups, members = depth_order.shape
    lanes = arrived.shape[2]
    sub = 2 * arrived.shape[1]
    tiles = arrived.reshape(devices // 2, sub, lanes)
    channels = colour_table.shape[0] + 1
    vmem = pl.BlockSpec(memory_space=pltpu.VMEM)
    return pl.pallas_call(
        functools.partial(render_kernel, members),
        out_shape=jax.ShapeDtypeStruct((channels, 2 * lanes), jnp.float32),
        in_specs=[vmem, vmem, vmem, pl.BlockSpec(memory_space=pltpu.SMEM)],
        out_specs=vmem,
        scratch_shapes=[pltpu.VMEM((channels, devices, sub, lanes), jnp.float32)],
    )(tiles, colour_table, opacity_table.reshape(1, -1), depth_order)


def exchange_kernel(send_ref, out_ref, landed, send_sem, recv_sem, own_sem):
    devices = send_ref.shape[0]
    members = lax.axis_size("tile")
    me = lax.axis_index("grp") * members + lax.axis_index("tile")

    def send(k, carry):
        dest = lax.rem(me + k, devices)
        pltpu.make_async_remote_copy(
            src_ref=send_ref.at[pl.ds(dest, 1)],
            dst_ref=landed.at[pl.ds(me, 1)],
            send_sem=send_sem,
            recv_sem=recv_sem,
            device_id=(dest // members, dest % members),
            device_id_type=pl.DeviceIdType.MESH,
        ).start()
        return carry

    lax.fori_loop(1, devices, send, 0)
    own = pltpu.make_async_copy(send_ref.at[pl.ds(me, 1)], landed.at[pl.ds(me, 1)], own_sem)
    own.start()
    own.wait()
    everything = pltpu.make_async_remote_copy(
        src_ref=send_ref.at[pl.ds(0, devices - 1)],
        dst_ref=landed.at[pl.ds(0, devices - 1)],
        send_sem=send_sem,
        recv_sem=recv_sem,
        device_id=(me // members, me % members),
        device_id_type=pl.DeviceIdType.MESH,
    )
    everything.wait_send()
    everything.wait_recv()
    out_ref[...] = landed[...]


def exchange(rows):
    return pl.pallas_call(
        exchange_kernel,
        out_shape=jax.ShapeDtypeStruct(rows.shape, rows.dtype),
        in_specs=[pl.BlockSpec(memory_space=pltpu.VMEM)],
        out_specs=pl.BlockSpec(memory_space=pltpu.VMEM),
        scratch_shapes=[
            pltpu.VMEM(rows.shape, rows.dtype),
            pltpu.SemaphoreType.DMA,
            pltpu.SemaphoreType.DMA,
            pltpu.SemaphoreType.DMA,
        ],
        compiler_params=pltpu.CompilerParams(has_side_effects=True),
    )(rows)


def body(bricks, colour_table, opacity_table, depth_order):
    groups = lax.axis_size("grp")
    members = lax.axis_size("tile")
    devices = groups * members
    depth = bricks.shape[0]
    pixels = bricks.shape[1] * bricks.shape[2]
    block = pixels // devices
    rows = jnp.transpose(bricks.reshape(depth, devices, block), (1, 0, 2))
    rows = rows.reshape(devices, depth * block // LANES, LANES)
    arrived = exchange(rows)
    return render(arrived, colour_table, opacity_table, depth_order)


def solution(mesh):
    in_specs = (P(("grp", "tile"), None, None), P(), P(), P())
    out_specs = P(None, ("grp", "tile"))
    return jax.shard_map(body, mesh=mesh, in_specs=in_specs, out_specs=out_specs, check_vma=False)
```

```python
import functools

import jax
import jax.numpy as jnp
from jax import lax
from jax.experimental import pallas as pl
from jax.experimental.pallas import tpu as pltpu
from jax.sharding import PartitionSpec as P

LANES = 128


def render_kernel(members, values_ref, colour_ref, opacity_ref, order_ref, out_ref, parts_ref):
    tiles, sub, lanes = values_ref.shape
    knots = colour_ref.shape[1]
    halves = knots // lanes
    colours = colour_ref.shape[0]
    groups = parts_ref.shape[1] // members
    rows = [colour_ref[c : c + 1, :] for c in range(colours)] + [opacity_ref[...]]
    tables = [
        [jnp.broadcast_to(r[:, h * lanes : (h + 1) * lanes], (sub, lanes)) for h in range(halves)]
        for r in rows
    ]
    last_lane = lax.broadcasted_iota(jnp.int32, (sub, lanes), 1) == lanes - 1
    uppers = []
    for per_half in tables:
        shifted = [pltpu.roll(x, lanes - 1, 1) for x in per_half]
        uppers.append(
            [jnp.where(last_lane, shifted[h + 1], shifted[h]) if h + 1 < halves else shifted[h] for h in range(halves)]
        )

    def pick(table, lane, in_half):
        got = jnp.take_along_axis(table[0], lane, axis=1, mode="promise_in_bounds")
        for h in range(1, halves):
            other = jnp.take_along_axis(table[h], lane, axis=1, mode="promise_in_bounds")
            got = jnp.where(in_half[h], other, got)
        return got

    def sample(v):
        u = v * float(knots - 1)
        lower = jnp.clip(jnp.floor(u), 0.0, float(knots - 2))
        frac = u - lower
        index = lower.astype(jnp.int32)
        lane = index % lanes
        half = index // lanes
        in_half = [None] + [half == h for h in range(1, halves)]
        return [
            pick(tables[c], lane, in_half) * (1.0 - frac) + pick(uppers[c], lane, in_half) * frac
            for c in range(colours + 1)
        ]

    def shade(m, carry):
        front = sample(values_ref[m])
        back = [pltpu.roll(x, sub - 2, 0) for x in front]
        a0 = front[colours]
        a1 = back[colours]
        colour = [a0 * front[c] for c in range(colours)]
        transmit = 1.0 - a0
        weight = transmit * a1
        colour = [colour[c] + weight * back[c] for c in range(colours)]
        transmit = transmit * (1.0 - a1)
        part = colour + [1.0 - transmit]
        for e in range(2):
            brick = 2 * m + e
            place = (brick // members) * members + order_ref[brick // members, brick % members]
            for c in range(colours + 1):
                parts_ref[c, place] = part[c] if e == 0 else pltpu.roll(part[c], sub - 4, 0)
        return carry

    lax.fori_loop(0, tiles, shade, 0, unroll=16)

    def blend(k, pics):
        out = []
        for g in range(groups):
            pic = pics[g]
            clear = 1.0 - pic[colours]
            out.append(tuple(pic[c] + clear * parts_ref[c, g * members + k] for c in range(colours + 1)))
        return tuple(out)

    zero = jnp.zeros((sub, lanes), jnp.float32)
    start = tuple(tuple(zero for _ in range(colours + 1)) for _ in range(groups))
    pics = lax.fori_loop(0, members, blend, start, unroll=4)
    final = pics[0]
    for g in range(1, groups):
        clear = 1.0 - final[colours]
        final = tuple(final[c] + clear * pics[g][c] for c in range(colours + 1))
    for c in range(colours + 1):
        for j in range(2):
            out_ref[c : c + 1, j * lanes : (j + 1) * lanes] = final[c][j : j + 1]


def render(arrived, colour_table, opacity_table, depth_order):
    devices = arrived.shape[0]
    groups, members = depth_order.shape
    lanes = arrived.shape[2]
    sub = 2 * arrived.shape[1]
    tiles = arrived.reshape(devices // 2, sub, lanes)
    channels = colour_table.shape[0] + 1
    vmem = pl.BlockSpec(memory_space=pltpu.VMEM)
    return pl.pallas_call(
        functools.partial(render_kernel, members),
        out_shape=jax.ShapeDtypeStruct((channels, 2 * lanes), jnp.float32),
        in_specs=[vmem, vmem, vmem, pl.BlockSpec(memory_space=pltpu.SMEM)],
        out_specs=vmem,
        scratch_shapes=[pltpu.VMEM((channels, devices, sub, lanes), jnp.float32)],
    )(tiles, colour_table, opacity_table.reshape(1, -1), depth_order)


def arrange_kernel(block, bricks_ref, out_ref):
    depth, height, width = bricks_ref.shape
    per_row = width // block
    parts = block // LANES
    chunk = depth * parts
    for s in range(depth):
        for col in range(width // LANES):
            h, j = divmod(col, parts)
            for r in range(0, height, 8):
                start = (per_row * r + h) * chunk + s * parts + j
                out_ref[pl.ds(start, 8, stride=per_row * chunk), :] = bricks_ref[s, pl.ds(r, 8), pl.ds(col * LANES, LANES)]


def arrange(bricks, devices):
    depth, height, width = bricks.shape
    block = height * width // devices
    vmem = pl.BlockSpec(memory_space=pltpu.VMEM)
    return pl.pallas_call(
        functools.partial(arrange_kernel, block),
        out_shape=jax.ShapeDtypeStruct((height * width * depth // LANES, LANES), bricks.dtype),
        in_specs=[vmem],
        out_specs=vmem,
    )(bricks)


def exchange_kernel(send_ref, out_ref, landed, send_sem, recv_sem, own_sem):
    devices, chunk, lanes = landed.shape
    members = lax.axis_size("tile")
    me = lax.axis_index("grp") * members + lax.axis_index("tile")

    def send(k, carry):
        dest = lax.rem(me + k, devices)
        pltpu.make_async_remote_copy(
            src_ref=send_ref.at[pl.ds(dest * chunk, chunk)],
            dst_ref=landed.at[me],
            send_sem=send_sem,
            recv_sem=recv_sem,
            device_id=(dest // members, dest % members),
            device_id_type=pl.DeviceIdType.MESH,
        ).start()
        return carry

    lax.fori_loop(1, devices, send, 0)
    own = pltpu.make_async_copy(send_ref.at[pl.ds(me * chunk, chunk)], landed.at[me], own_sem)
    own.start()
    own.wait()
    everything = pltpu.make_async_remote_copy(
        src_ref=landed.at[pl.ds(0, devices - 1)],
        dst_ref=landed.at[pl.ds(0, devices - 1)],
        send_sem=send_sem,
        recv_sem=recv_sem,
        device_id=(me // members, me % members),
        device_id_type=pl.DeviceIdType.MESH,
    )
    everything.wait_send()
    everything.wait_recv()
    out_ref[...] = landed[...]


def exchange(flat, devices):
    chunk = flat.shape[0] // devices
    shape = (devices, chunk, flat.shape[1])
    return pl.pallas_call(
        exchange_kernel,
        out_shape=jax.ShapeDtypeStruct(shape, flat.dtype),
        in_specs=[pl.BlockSpec(memory_space=pltpu.VMEM)],
        out_specs=pl.BlockSpec(memory_space=pltpu.VMEM),
        scratch_shapes=[
            pltpu.VMEM(shape, flat.dtype),
            pltpu.SemaphoreType.DMA,
            pltpu.SemaphoreType.DMA,
            pltpu.SemaphoreType.DMA,
        ],
        compiler_params=pltpu.CompilerParams(has_side_effects=True),
    )(flat)


def body(bricks, colour_table, opacity_table, depth_order):
    groups = lax.axis_size("grp")
    members = lax.axis_size("tile")
    devices = groups * members
    flat = arrange(bricks, devices)
    arrived = exchange(flat, devices)
    return render(arrived, colour_table, opacity_table, depth_order)


def solution(mesh):
    in_specs = (P(("grp", "tile"), None, None), P(), P(), P())
    out_specs = P(None, ("grp", "tile"))
    return jax.shard_map(body, mesh=mesh, in_specs=in_specs, out_specs=out_specs, check_vma=False)
```

```python
import functools

import jax
import jax.numpy as jnp
from jax import lax
from jax.experimental import pallas as pl
from jax.experimental.pallas import tpu as pltpu
from jax.sharding import PartitionSpec as P

LANES = 128


def render_kernel(members, values_ref, colour_ref, opacity_ref, order_ref, out_ref, parts_ref):
    tiles, sub, lanes = values_ref.shape
    knots = colour_ref.shape[1]
    halves = knots // lanes
    colours = colour_ref.shape[0]
    groups = parts_ref.shape[1] // members
    rows = [colour_ref[c : c + 1, :] for c in range(colours)] + [opacity_ref[...]]
    tables = [
        [jnp.broadcast_to(r[:, h * lanes : (h + 1) * lanes], (sub, lanes)) for h in range(halves)]
        for r in rows
    ]
    last_lane = lax.broadcasted_iota(jnp.int32, (sub, lanes), 1) == lanes - 1
    uppers = []
    for per_half in tables:
        shifted = [pltpu.roll(x, lanes - 1, 1) for x in per_half]
        uppers.append(
            [jnp.where(last_lane, shifted[h + 1], shifted[h]) if h + 1 < halves else shifted[h] for h in range(halves)]
        )

    def pick(table, lane, in_half):
        got = jnp.take_along_axis(table[0], lane, axis=1, mode="promise_in_bounds")
        for h in range(1, halves):
            other = jnp.take_along_axis(table[h], lane, axis=1, mode="promise_in_bounds")
            got = jnp.where(in_half[h], other, got)
        return got

    def sample(v):
        u = v * float(knots - 1)
        lower = jnp.clip(jnp.floor(u), 0.0, float(knots - 2))
        frac = u - lower
        index = lower.astype(jnp.int32)
        lane = index % lanes
        half = index // lanes
        in_half = [None] + [half == h for h in range(1, halves)]
        return [
            pick(tables[c], lane, in_half) * (1.0 - frac) + pick(uppers[c], lane, in_half) * frac
            for c in range(colours + 1)
        ]

    def shade(m, carry):
        front = sample(values_ref[m])
        back = [pltpu.roll(x, sub - 2, 0) for x in front]
        a0 = front[colours]
        a1 = back[colours]
        colour = [a0 * front[c] for c in range(colours)]
        transmit = 1.0 - a0
        weight = transmit * a1
        colour = [colour[c] + weight * back[c] for c in range(colours)]
        transmit = transmit * (1.0 - a1)
        part = colour + [1.0 - transmit]
        for e in range(2):
            brick = 2 * m + e
            place = (brick // members) * members + order_ref[brick // members, brick % members]
            for c in range(colours + 1):
                parts_ref[c, place] = part[c] if e == 0 else pltpu.roll(part[c], sub - 4, 0)
        return carry

    lax.fori_loop(0, tiles, shade, 0, unroll=32)

    def blend(k, pics):
        out = []
        for g in range(groups):
            pic = pics[g]
            clear = 1.0 - pic[colours]
            out.append(tuple(pic[c] + clear * parts_ref[c, g * members + k] for c in range(colours + 1)))
        return tuple(out)

    zero = jnp.zeros((sub, lanes), jnp.float32)
    start = tuple(tuple(zero for _ in range(colours + 1)) for _ in range(groups))
    pics = lax.fori_loop(0, members, blend, start, unroll=8)
    final = pics[0]
    for g in range(1, groups):
        clear = 1.0 - final[colours]
        final = tuple(final[c] + clear * pics[g][c] for c in range(colours + 1))
    for c in range(colours + 1):
        for j in range(2):
            out_ref[c : c + 1, j * lanes : (j + 1) * lanes] = final[c][j : j + 1]


def render(arrived, colour_table, opacity_table, depth_order):
    devices = arrived.shape[0]
    groups, members = depth_order.shape
    lanes = arrived.shape[2]
    sub = 2 * arrived.shape[1]
    tiles = arrived.reshape(devices // 2, sub, lanes)
    channels = colour_table.shape[0] + 1
    vmem = pl.BlockSpec(memory_space=pltpu.VMEM)
    return pl.pallas_call(
        functools.partial(render_kernel, members),
        out_shape=jax.ShapeDtypeStruct((channels, 2 * lanes), jnp.float32),
        in_specs=[vmem, vmem, vmem, pl.BlockSpec(memory_space=pltpu.SMEM)],
        out_specs=vmem,
        scratch_shapes=[pltpu.VMEM((channels, devices, sub, lanes), jnp.float32)],
    )(tiles, colour_table, opacity_table.reshape(1, -1), depth_order)


def arrange_kernel(block, bricks_ref, out_ref):
    depth, height, width = bricks_ref.shape
    per_row = width // block
    parts = block // LANES
    chunk = depth * parts
    for s in range(depth):
        for col in range(width // LANES):
            h, j = divmod(col, parts)
            for r in range(0, height, 8):
                start = (per_row * r + h) * chunk + s * parts + j
                out_ref[pl.ds(start, 8, stride=per_row * chunk), :] = bricks_ref[s, pl.ds(r, 8), pl.ds(col * LANES, LANES)]


def arrange(bricks, devices):
    depth, height, width = bricks.shape
    block = height * width // devices
    vmem = pl.BlockSpec(memory_space=pltpu.VMEM)
    return pl.pallas_call(
        functools.partial(arrange_kernel, block),
        out_shape=jax.ShapeDtypeStruct((height * width * depth // LANES, LANES), bricks.dtype),
        in_specs=[vmem],
        out_specs=vmem,
    )(bricks)


def exchange_kernel(send_ref, out_ref, landed, send_sem, recv_sem, own_sem):
    devices, chunk, lanes = landed.shape
    members = lax.axis_size("tile")
    me = lax.axis_index("grp") * members + lax.axis_index("tile")

    def send(k, carry):
        dest = lax.rem(me + k, devices)
        pltpu.make_async_remote_copy(
            src_ref=send_ref.at[pl.ds(dest * chunk, chunk)],
            dst_ref=landed.at[me],
            send_sem=send_sem,
            recv_sem=recv_sem,
            device_id=(dest // members, dest % members),
            device_id_type=pl.DeviceIdType.MESH,
        ).start()
        return carry

    lax.fori_loop(1, devices, send, 0)
    own = pltpu.make_async_copy(send_ref.at[pl.ds(me * chunk, chunk)], landed.at[me], own_sem)
    own.start()
    own.wait()
    everything = pltpu.make_async_remote_copy(
        src_ref=landed.at[pl.ds(0, devices - 1)],
        dst_ref=landed.at[pl.ds(0, devices - 1)],
        send_sem=send_sem,
        recv_sem=recv_sem,
        device_id=(me // members, me % members),
        device_id_type=pl.DeviceIdType.MESH,
    )
    everything.wait_send()
    everything.wait_recv()
    out_ref[...] = landed[...]


def exchange(flat, devices):
    chunk = flat.shape[0] // devices
    shape = (devices, chunk, flat.shape[1])
    return pl.pallas_call(
        exchange_kernel,
        out_shape=jax.ShapeDtypeStruct(shape, flat.dtype),
        in_specs=[pl.BlockSpec(memory_space=pltpu.VMEM)],
        out_specs=pl.BlockSpec(memory_space=pltpu.VMEM),
        scratch_shapes=[
            pltpu.VMEM(shape, flat.dtype),
            pltpu.SemaphoreType.DMA,
            pltpu.SemaphoreType.DMA,
            pltpu.SemaphoreType.DMA,
        ],
        compiler_params=pltpu.CompilerParams(has_side_effects=True),
    )(flat)


def body(bricks, colour_table, opacity_table, depth_order):
    groups = lax.axis_size("grp")
    members = lax.axis_size("tile")
    devices = groups * members
    flat = arrange(bricks, devices)
    arrived = exchange(flat, devices)
    return render(arrived, colour_table, opacity_table, depth_order)


def solution(mesh):
    in_specs = (P(("grp", "tile"), None, None), P(), P(), P())
    out_specs = P(None, ("grp", "tile"))
    return jax.shard_map(body, mesh=mesh, in_specs=in_specs, out_specs=out_specs, check_vma=False)
```

```python
import functools

import jax
import jax.numpy as jnp
from jax import lax
from jax.experimental import pallas as pl
from jax.experimental.pallas import tpu as pltpu
from jax.sharding import PartitionSpec as P

LANES = 128


def render_kernel(members, values_ref, colour_ref, opacity_ref, order_ref, out_ref, parts_ref):
    tiles, sub, lanes = values_ref.shape
    knots = colour_ref.shape[1]
    halves = knots // lanes
    colours = colour_ref.shape[0]
    groups = parts_ref.shape[1] // members
    rows = [colour_ref[c : c + 1, :] for c in range(colours)] + [opacity_ref[...]]
    tables = [
        [jnp.broadcast_to(r[:, h * lanes : (h + 1) * lanes], (sub, lanes)) for h in range(halves)]
        for r in rows
    ]
    last_lane = lax.broadcasted_iota(jnp.int32, (sub, lanes), 1) == lanes - 1
    uppers = []
    for per_half in tables:
        shifted = [pltpu.roll(x, lanes - 1, 1) for x in per_half]
        uppers.append(
            [jnp.where(last_lane, shifted[h + 1], shifted[h]) if h + 1 < halves else shifted[h] for h in range(halves)]
        )

    def pick(table, lane, in_half):
        got = jnp.take_along_axis(table[0], lane, axis=1, mode="promise_in_bounds")
        for h in range(1, halves):
            other = jnp.take_along_axis(table[h], lane, axis=1, mode="promise_in_bounds")
            got = jnp.where(in_half[h], other, got)
        return got

    def sample(v):
        u = v * float(knots - 1)
        lower = jnp.clip(jnp.floor(u), 0.0, float(knots - 2))
        frac = u - lower
        index = lower.astype(jnp.int32)
        lane = index % lanes
        half = index // lanes
        in_half = [None] + [half == h for h in range(1, halves)]
        return [
            pick(tables[c], lane, in_half) * (1.0 - frac) + pick(uppers[c], lane, in_half) * frac
            for c in range(colours + 1)
        ]

    def shade(m, carry):
        front = sample(values_ref[m])
        back = [pltpu.roll(x, sub - 2, 0) for x in front]
        a0 = front[colours]
        a1 = back[colours]
        colour = [a0 * front[c] for c in range(colours)]
        transmit = 1.0 - a0
        weight = transmit * a1
        colour = [colour[c] + weight * back[c] for c in range(colours)]
        transmit = transmit * (1.0 - a1)
        part = colour + [1.0 - transmit]
        for e in range(2):
            brick = 2 * m + e
            place = (brick // members) * members + order_ref[brick // members, brick % members]
            for c in range(colours + 1):
                parts_ref[c, place] = part[c] if e == 0 else pltpu.roll(part[c], sub - 4, 0)
        return carry

    lax.fori_loop(0, tiles, shade, 0, unroll=32)

    def blend(k, pics):
        out = []
        for g in range(groups):
            pic = pics[g]
            clear = 1.0 - pic[colours]
            out.append(tuple(pic[c] + clear * parts_ref[c, g * members + k] for c in range(colours + 1)))
        return tuple(out)

    zero = jnp.zeros((sub, lanes), jnp.float32)
    start = tuple(tuple(zero for _ in range(colours + 1)) for _ in range(groups))
    pics = lax.fori_loop(0, members, blend, start, unroll=8)
    final = pics[0]
    for g in range(1, groups):
        clear = 1.0 - final[colours]
        final = tuple(final[c] + clear * pics[g][c] for c in range(colours + 1))
    for c in range(colours + 1):
        for j in range(2):
            out_ref[c : c + 1, j * lanes : (j + 1) * lanes] = final[c][j : j + 1]


def render(arrived, colour_table, opacity_table, depth_order):
    devices = arrived.shape[0]
    groups, members = depth_order.shape
    lanes = arrived.shape[2]
    sub = 2 * arrived.shape[1]
    tiles = arrived.reshape(devices // 2, sub, lanes)
    channels = colour_table.shape[0] + 1
    vmem = pl.BlockSpec(memory_space=pltpu.VMEM)
    return pl.pallas_call(
        functools.partial(render_kernel, members),
        out_shape=jax.ShapeDtypeStruct((channels, 2 * lanes), jnp.float32),
        in_specs=[vmem, vmem, vmem, pl.BlockSpec(memory_space=pltpu.SMEM)],
        out_specs=vmem,
        scratch_shapes=[pltpu.VMEM((channels, devices, sub, lanes), jnp.float32)],
    )(tiles, colour_table, opacity_table.reshape(1, -1), depth_order)


def arrange_kernel(block, bricks_ref, out_ref):
    depth, height, width = bricks_ref.shape
    per_row = width // block
    parts = block // LANES
    chunk = depth * parts
    for s in range(depth):
        for col in range(width // LANES):
            h, j = divmod(col, parts)
            for r in range(0, height, 8):
                start = (per_row * r + h) * chunk + s * parts + j
                out_ref[pl.ds(start, 8, stride=per_row * chunk), :] = bricks_ref[s, pl.ds(r, 8), pl.ds(col * LANES, LANES)]


def arrange(bricks, devices):
    depth, height, width = bricks.shape
    block = height * width // devices
    vmem = pl.BlockSpec(memory_space=pltpu.VMEM)
    return pl.pallas_call(
        functools.partial(arrange_kernel, block),
        out_shape=jax.ShapeDtypeStruct((height * width * depth // LANES, LANES), bricks.dtype),
        in_specs=[vmem],
        out_specs=vmem,
    )(bricks)


def exchange_kernel(send_ref, out_ref, landed, send_sem, recv_sem, own_sem):
    devices, chunk, lanes = landed.shape
    members = lax.axis_size("tile")
    me = lax.axis_index("grp") * members + lax.axis_index("tile")

    groups = devices // members
    g = lax.axis_index("grp")
    t = lax.axis_index("tile")

    def send(k, carry):
        peer_g = lax.rem(g + k % groups, groups)
        peer_t = lax.rem(t + k // groups, members)
        dest = peer_g * members + peer_t
        pltpu.make_async_remote_copy(
            src_ref=send_ref.at[pl.ds(dest * chunk, chunk)],
            dst_ref=landed.at[me],
            send_sem=send_sem,
            recv_sem=recv_sem,
            device_id=(peer_g, peer_t),
            device_id_type=pl.DeviceIdType.MESH,
        ).start()
        return carry

    lax.fori_loop(1, devices, send, 0)
    own = pltpu.make_async_copy(send_ref.at[pl.ds(me * chunk, chunk)], landed.at[me], own_sem)
    own.start()
    own.wait()
    everything = pltpu.make_async_remote_copy(
        src_ref=landed.at[pl.ds(0, devices - 1)],
        dst_ref=landed.at[pl.ds(0, devices - 1)],
        send_sem=send_sem,
        recv_sem=recv_sem,
        device_id=(me // members, me % members),
        device_id_type=pl.DeviceIdType.MESH,
    )
    everything.wait_send()
    everything.wait_recv()
    out_ref[...] = landed[...]


def exchange(flat, devices):
    chunk = flat.shape[0] // devices
    shape = (devices, chunk, flat.shape[1])
    return pl.pallas_call(
        exchange_kernel,
        out_shape=jax.ShapeDtypeStruct(shape, flat.dtype),
        in_specs=[pl.BlockSpec(memory_space=pltpu.VMEM)],
        out_specs=pl.BlockSpec(memory_space=pltpu.VMEM),
        scratch_shapes=[
            pltpu.VMEM(shape, flat.dtype),
            pltpu.SemaphoreType.DMA,
            pltpu.SemaphoreType.DMA,
            pltpu.SemaphoreType.DMA,
        ],
        compiler_params=pltpu.CompilerParams(has_side_effects=True),
    )(flat)


def body(bricks, colour_table, opacity_table, depth_order):
    groups = lax.axis_size("grp")
    members = lax.axis_size("tile")
    devices = groups * members
    flat = arrange(bricks, devices)
    arrived = exchange(flat, devices)
    return render(arrived, colour_table, opacity_table, depth_order)


def solution(mesh):
    in_specs = (P(("grp", "tile"), None, None), P(), P(), P())
    out_specs = P(None, ("grp", "tile"))
    return jax.shard_map(body, mesh=mesh, in_specs=in_specs, out_specs=out_specs, check_vma=False)
```

```python
import functools

import jax
import jax.numpy as jnp
from jax import lax
from jax.experimental import pallas as pl
from jax.experimental.pallas import tpu as pltpu
from jax.sharding import PartitionSpec as P

LANES = 128


def render_kernel(members, values_ref, colour_ref, opacity_ref, order_ref, out_ref, parts_ref):
    tiles, sub, lanes = values_ref.shape
    knots = colour_ref.shape[1]
    halves = knots // lanes
    colours = colour_ref.shape[0]
    groups = parts_ref.shape[1] // members
    rows = [colour_ref[c : c + 1, :] for c in range(colours)] + [opacity_ref[...]]
    tables = [
        [jnp.broadcast_to(r[:, h * lanes : (h + 1) * lanes], (sub, lanes)) for h in range(halves)]
        for r in rows
    ]
    last_lane = lax.broadcasted_iota(jnp.int32, (sub, lanes), 1) == lanes - 1
    uppers = []
    for per_half in tables:
        shifted = [pltpu.roll(x, lanes - 1, 1) for x in per_half]
        uppers.append(
            [jnp.where(last_lane, shifted[h + 1], shifted[h]) if h + 1 < halves else shifted[h] for h in range(halves)]
        )

    def pick(table, lane, in_half):
        got = jnp.take_along_axis(table[0], lane, axis=1, mode="promise_in_bounds")
        for h in range(1, halves):
            other = jnp.take_along_axis(table[h], lane, axis=1, mode="promise_in_bounds")
            got = jnp.where(in_half[h], other, got)
        return got

    def sample(v):
        u = v * float(knots - 1)
        lower = jnp.clip(jnp.floor(u), 0.0, float(knots - 2))
        frac = u - lower
        index = lower.astype(jnp.int32)
        lane = index % lanes
        half = index // lanes
        in_half = [None] + [half == h for h in range(1, halves)]
        return [
            pick(tables[c], lane, in_half) * (1.0 - frac) + pick(uppers[c], lane, in_half) * frac
            for c in range(colours + 1)
        ]

    def shade(m, carry):
        front = sample(values_ref[m])
        back = [pltpu.roll(x, sub - 2, 0) for x in front]
        a0 = front[colours]
        a1 = back[colours]
        colour = [a0 * front[c] for c in range(colours)]
        transmit = 1.0 - a0
        weight = transmit * a1
        colour = [colour[c] + weight * back[c] for c in range(colours)]
        transmit = transmit * (1.0 - a1)
        part = colour + [1.0 - transmit]
        for e in range(2):
            brick = 2 * m + e
            place = (brick // members) * members + order_ref[brick // members, brick % members]
            for c in range(colours + 1):
                parts_ref[c, place] = part[c] if e == 0 else pltpu.roll(part[c], sub - 4, 0)
        return carry

    lax.fori_loop(0, tiles, shade, 0, unroll=32)

    def blend(k, pics):
        out = []
        for g in range(groups):
            pic = pics[g]
            clear = 1.0 - pic[colours]
            out.append(tuple(pic[c] + clear * parts_ref[c, g * members + k] for c in range(colours + 1)))
        return tuple(out)

    zero = jnp.zeros((sub, lanes), jnp.float32)
    start = tuple(tuple(zero for _ in range(colours + 1)) for _ in range(groups))
    pics = lax.fori_loop(0, members, blend, start, unroll=8)
    final = pics[0]
    for g in range(1, groups):
        clear = 1.0 - final[colours]
        final = tuple(final[c] + clear * pics[g][c] for c in range(colours + 1))
    for c in range(colours + 1):
        for j in range(2):
            out_ref[c : c + 1, j * lanes : (j + 1) * lanes] = final[c][j : j + 1]


def render(arrived, colour_table, opacity_table, depth_order):
    pairs, sub, lanes = arrived.shape
    devices = 2 * pairs
    groups, members = depth_order.shape
    tiles = arrived
    channels = colour_table.shape[0] + 1
    vmem = pl.BlockSpec(memory_space=pltpu.VMEM)
    return pl.pallas_call(
        functools.partial(render_kernel, members),
        out_shape=jax.ShapeDtypeStruct((channels, 2 * lanes), jnp.float32),
        in_specs=[vmem, vmem, vmem, pl.BlockSpec(memory_space=pltpu.SMEM)],
        out_specs=vmem,
        scratch_shapes=[pltpu.VMEM((channels, devices, sub, lanes), jnp.float32)],
    )(tiles, colour_table, opacity_table.reshape(1, -1), depth_order)


def arrange_kernel(block, bricks_ref, out_ref):
    depth, height, width = bricks_ref.shape
    per_row = width // block
    parts = block // LANES
    chunk = depth * parts
    for s in range(depth):
        for col in range(width // LANES):
            h, j = divmod(col, parts)
            for r in range(0, height, 8):
                start = (per_row * r + h) * chunk + s * parts + j
                out_ref[pl.ds(start, 8, stride=per_row * chunk), :] = bricks_ref[s, pl.ds(r, 8), pl.ds(col * LANES, LANES)]


def arrange(bricks, devices):
    depth, height, width = bricks.shape
    block = height * width // devices
    vmem = pl.BlockSpec(memory_space=pltpu.VMEM)
    return pl.pallas_call(
        functools.partial(arrange_kernel, block),
        out_shape=jax.ShapeDtypeStruct((height * width * depth // LANES, LANES), bricks.dtype),
        in_specs=[vmem],
        out_specs=vmem,
    )(bricks)


def exchange_kernel(send_ref, out_ref, middle, landed, sems):
    pairs, sub, lanes = send_ref.shape
    half = sub // 2
    members = lax.axis_size("tile")
    pair_members = members // 2
    groups = pairs // pair_members
    g = lax.axis_index("grp")
    t = lax.axis_index("tile")
    core = t % 2
    mine = (g * members + t) // 2
    send1, recv1, send2, recv2, own1, own2 = (sems.at[i] for i in range(6))
    partner = pltpu.make_async_remote_copy(
        src_ref=send_ref.at[:, pl.ds((1 - core) * half, half), :],
        dst_ref=middle.at[:, pl.ds(core * half, half), :],
        send_sem=send1,
        recv_sem=recv1,
        device_id=(g, t + 1 - 2 * core),
        device_id_type=pl.DeviceIdType.MESH,
    )
    partner.start()
    kept = pltpu.make_async_copy(
        send_ref.at[:, pl.ds(core * half, half), :], middle.at[:, pl.ds(core * half, half), :], own1
    )
    kept.start()
    kept.wait()
    partner.wait_recv()

    def send(k, carry):
        peer_g = lax.rem(g + k % groups, groups)
        peer_p = lax.rem(t // 2 + k // groups, pair_members)
        pltpu.make_async_remote_copy(
            src_ref=middle.at[peer_g * pair_members + peer_p],
            dst_ref=landed.at[mine],
            send_sem=send2,
            recv_sem=recv2,
            device_id=(peer_g, 2 * peer_p + core),
            device_id_type=pl.DeviceIdType.MESH,
        ).start()
        return carry

    lax.fori_loop(1, pairs, send, 0)
    local = pltpu.make_async_copy(middle.at[mine], landed.at[mine], own2)
    local.start()
    local.wait()
    everything = pltpu.make_async_remote_copy(
        src_ref=landed.at[pl.ds(0, pairs - 1)],
        dst_ref=landed.at[pl.ds(0, pairs - 1)],
        send_sem=send2,
        recv_sem=recv2,
        device_id=(g, t),
        device_id_type=pl.DeviceIdType.MESH,
    )
    everything.wait_recv()
    partner.wait_send()
    everything.wait_send()
    out_ref[...] = landed[...]


def exchange(flat, devices):
    sub = 2 * flat.shape[0] // devices
    shape = (devices // 2, sub, flat.shape[1])
    return pl.pallas_call(
        exchange_kernel,
        out_shape=jax.ShapeDtypeStruct(shape, flat.dtype),
        in_specs=[pl.BlockSpec(memory_space=pltpu.VMEM)],
        out_specs=pl.BlockSpec(memory_space=pltpu.VMEM),
        scratch_shapes=[
            pltpu.VMEM(shape, flat.dtype),
            pltpu.VMEM(shape, flat.dtype),
            pltpu.SemaphoreType.DMA((6,)),
        ],
        compiler_params=pltpu.CompilerParams(has_side_effects=True),
    )(flat.reshape(shape))


def body(bricks, colour_table, opacity_table, depth_order):
    groups = lax.axis_size("grp")
    members = lax.axis_size("tile")
    devices = groups * members
    flat = arrange(bricks, devices)
    arrived = exchange(flat, devices)
    return render(arrived, colour_table, opacity_table, depth_order)


def solution(mesh):
    in_specs = (P(("grp", "tile"), None, None), P(), P(), P())
    out_specs = P(None, ("grp", "tile"))
    return jax.shard_map(body, mesh=mesh, in_specs=in_specs, out_specs=out_specs, check_vma=False)
```

```python
import functools

import jax
import jax.numpy as jnp
from jax import lax
from jax.experimental import pallas as pl
from jax.experimental.pallas import tpu as pltpu
from jax.sharding import PartitionSpec as P

LANES = 128


def render_kernel(members, values_ref, colour_ref, opacity_ref, order_ref, out_ref, parts_ref):
    tiles, sub, lanes = values_ref.shape
    knots = colour_ref.shape[1]
    halves = knots // lanes
    colours = colour_ref.shape[0]
    groups = parts_ref.shape[1] // members
    rows = [colour_ref[c : c + 1, :] for c in range(colours)] + [opacity_ref[...]]
    tables = [
        [jnp.broadcast_to(r[:, h * lanes : (h + 1) * lanes], (sub, lanes)) for h in range(halves)]
        for r in rows
    ]
    last_lane = lax.broadcasted_iota(jnp.int32, (sub, lanes), 1) == lanes - 1
    uppers = []
    for per_half in tables:
        shifted = [pltpu.roll(x, lanes - 1, 1) for x in per_half]
        uppers.append(
            [jnp.where(last_lane, shifted[h + 1], shifted[h]) if h + 1 < halves else shifted[h] for h in range(halves)]
        )

    def pick(table, lane, in_half):
        got = jnp.take_along_axis(table[0], lane, axis=1, mode="promise_in_bounds")
        for h in range(1, halves):
            other = jnp.take_along_axis(table[h], lane, axis=1, mode="promise_in_bounds")
            got = jnp.where(in_half[h], other, got)
        return got

    def sample(v):
        u = v * float(knots - 1)
        lower = jnp.clip(jnp.floor(u), 0.0, float(knots - 2))
        frac = u - lower
        index = lower.astype(jnp.int32)
        lane = index % lanes
        half = index // lanes
        in_half = [None] + [half == h for h in range(1, halves)]
        return [
            pick(tables[c], lane, in_half) * (1.0 - frac) + pick(uppers[c], lane, in_half) * frac
            for c in range(colours + 1)
        ]

    def shade(m, carry):
        front = sample(values_ref[m])
        back = [pltpu.roll(x, sub - 2, 0) for x in front]
        a0 = front[colours]
        a1 = back[colours]
        colour = [a0 * front[c] for c in range(colours)]
        transmit = 1.0 - a0
        weight = transmit * a1
        colour = [colour[c] + weight * back[c] for c in range(colours)]
        transmit = transmit * (1.0 - a1)
        part = colour + [1.0 - transmit]
        for e in range(2):
            brick = 2 * m + e
            place = (brick // members) * members + order_ref[brick // members, brick % members]
            for c in range(colours + 1):
                parts_ref[c, place] = part[c] if e == 0 else pltpu.roll(part[c], sub - 4, 0)
        return carry

    lax.fori_loop(0, tiles, shade, 0, unroll=32)

    def blend(k, pics):
        out = []
        for g in range(groups):
            pic = pics[g]
            clear = 1.0 - pic[colours]
            out.append(tuple(pic[c] + clear * parts_ref[c, g * members + k] for c in range(colours + 1)))
        return tuple(out)

    zero = jnp.zeros((sub, lanes), jnp.float32)
    start = tuple(tuple(zero for _ in range(colours + 1)) for _ in range(groups))
    pics = lax.fori_loop(0, members, blend, start, unroll=8)
    final = pics[0]
    for g in range(1, groups):
        clear = 1.0 - final[colours]
        final = tuple(final[c] + clear * pics[g][c] for c in range(colours + 1))
    for c in range(colours + 1):
        for j in range(2):
            out_ref[c : c + 1, j * lanes : (j + 1) * lanes] = final[c][j : j + 1]


def render(arrived, colour_table, opacity_table, depth_order):
    devices = arrived.shape[0]
    groups, members = depth_order.shape
    lanes = arrived.shape[2]
    sub = 2 * arrived.shape[1]
    tiles = arrived.reshape(devices // 2, sub, lanes)
    channels = colour_table.shape[0] + 1
    vmem = pl.BlockSpec(memory_space=pltpu.VMEM)
    return pl.pallas_call(
        functools.partial(render_kernel, members),
        out_shape=jax.ShapeDtypeStruct((channels, 2 * lanes), jnp.float32),
        in_specs=[vmem, vmem, vmem, pl.BlockSpec(memory_space=pltpu.SMEM)],
        out_specs=vmem,
        scratch_shapes=[pltpu.VMEM((channels, devices, sub, lanes), jnp.float32)],
    )(tiles, colour_table, opacity_table.reshape(1, -1), depth_order)


def arrange_kernel(block, bricks_ref, out_ref):
    depth, height, width = bricks_ref.shape
    per_row = width // block
    parts = block // LANES
    chunk = depth * parts
    for s in range(depth):
        for col in range(width // LANES):
            h, j = divmod(col, parts)
            for r in range(0, height, 8):
                start = (per_row * r + h) * chunk + s * parts + j
                out_ref[pl.ds(start, 8, stride=per_row * chunk), :] = bricks_ref[s, pl.ds(r, 8), pl.ds(col * LANES, LANES)]


def arrange(bricks, devices):
    depth, height, width = bricks.shape
    block = height * width // devices
    vmem = pl.BlockSpec(memory_space=pltpu.VMEM)
    return pl.pallas_call(
        functools.partial(arrange_kernel, block),
        out_shape=jax.ShapeDtypeStruct((height * width * depth // LANES, LANES), bricks.dtype),
        in_specs=[vmem],
        out_specs=vmem,
    )(bricks)


def exchange_kernel(send_ref, out_ref, landed, send_sem, recv_sem, own_sem):
    devices, chunk, lanes = landed.shape
    members = lax.axis_size("tile")
    me = lax.axis_index("grp") * members + lax.axis_index("tile")

    groups = devices // members
    g = lax.axis_index("grp")
    t = lax.axis_index("tile")

    def peer(k):
        return lax.rem(g + k % groups, groups), lax.rem(t + k // groups, members)

    barrier = pltpu.get_barrier_semaphore()

    def greet(k, carry):
        pl.semaphore_signal(barrier, 1, device_id=peer(k), device_id_type=pl.DeviceIdType.MESH)
        return carry

    lax.fori_loop(1, devices, greet, 0)
    pl.semaphore_wait(barrier, devices - 1)

    def send(k, carry):
        peer_g, peer_t = peer(k)
        dest = peer_g * members + peer_t
        pltpu.make_async_remote_copy(
            src_ref=send_ref.at[pl.ds(dest * chunk, chunk)],
            dst_ref=landed.at[me],
            send_sem=send_sem,
            recv_sem=recv_sem,
            device_id=(peer_g, peer_t),
            device_id_type=pl.DeviceIdType.MESH,
        ).start()
        return carry

    lax.fori_loop(1, devices, send, 0)
    own = pltpu.make_async_copy(send_ref.at[pl.ds(me * chunk, chunk)], landed.at[me], own_sem)
    own.start()
    own.wait()
    everything = pltpu.make_async_remote_copy(
        src_ref=landed.at[pl.ds(0, devices - 1)],
        dst_ref=landed.at[pl.ds(0, devices - 1)],
        send_sem=send_sem,
        recv_sem=recv_sem,
        device_id=(me // members, me % members),
        device_id_type=pl.DeviceIdType.MESH,
    )
    everything.wait_send()
    everything.wait_recv()
    out_ref[...] = landed[...]


def exchange(flat, devices):
    chunk = flat.shape[0] // devices
    shape = (devices, chunk, flat.shape[1])
    return pl.pallas_call(
        exchange_kernel,
        out_shape=jax.ShapeDtypeStruct(shape, flat.dtype),
        in_specs=[pl.BlockSpec(memory_space=pltpu.VMEM)],
        out_specs=pl.BlockSpec(memory_space=pltpu.VMEM),
        scratch_shapes=[
            pltpu.VMEM(shape, flat.dtype),
            pltpu.SemaphoreType.DMA,
            pltpu.SemaphoreType.DMA,
            pltpu.SemaphoreType.DMA,
        ],
        compiler_params=pltpu.CompilerParams(collective_id=0, has_side_effects=True),
    )(flat)


def body(bricks, colour_table, opacity_table, depth_order):
    groups = lax.axis_size("grp")
    members = lax.axis_size("tile")
    devices = groups * members
    flat = arrange(bricks, devices)
    arrived = exchange(flat, devices)
    return render(arrived, colour_table, opacity_table, depth_order)


def solution(mesh):
    in_specs = (P(("grp", "tile"), None, None), P(), P(), P())
    out_specs = P(None, ("grp", "tile"))
    return jax.shard_map(body, mesh=mesh, in_specs=in_specs, out_specs=out_specs, check_vma=False)
```

```python
import functools

import jax
import jax.numpy as jnp
from jax import lax
from jax.experimental import pallas as pl
from jax.experimental.pallas import tpu as pltpu
from jax.sharding import PartitionSpec as P

LANES = 128


def render_kernel(members, values_ref, colour_ref, opacity_ref, order_ref, out_ref, parts_ref):
    tiles, sub, lanes = values_ref.shape
    knots = colour_ref.shape[1]
    halves = knots // lanes
    colours = colour_ref.shape[0]
    groups = parts_ref.shape[1] // members
    rows = [colour_ref[c : c + 1, :] for c in range(colours)] + [opacity_ref[...]]
    tables = [
        [jnp.broadcast_to(r[:, h * lanes : (h + 1) * lanes], (sub, lanes)) for h in range(halves)]
        for r in rows
    ]
    last_lane = lax.broadcasted_iota(jnp.int32, (sub, lanes), 1) == lanes - 1
    uppers = []
    for per_half in tables:
        shifted = [pltpu.roll(x, lanes - 1, 1) for x in per_half]
        uppers.append(
            [jnp.where(last_lane, shifted[h + 1], shifted[h]) if h + 1 < halves else shifted[h] for h in range(halves)]
        )

    def pick(table, lane, in_half):
        got = jnp.take_along_axis(table[0], lane, axis=1, mode="promise_in_bounds")
        for h in range(1, halves):
            other = jnp.take_along_axis(table[h], lane, axis=1, mode="promise_in_bounds")
            got = jnp.where(in_half[h], other, got)
        return got

    def sample(v):
        u = v * float(knots - 1)
        lower = jnp.clip(jnp.floor(u), 0.0, float(knots - 2))
        frac = u - lower
        index = lower.astype(jnp.int32)
        lane = index % lanes
        half = index // lanes
        in_half = [None] + [half == h for h in range(1, halves)]
        return [
            pick(tables[c], lane, in_half) * (1.0 - frac) + pick(uppers[c], lane, in_half) * frac
            for c in range(colours + 1)
        ]

    def shade(m, carry):
        front = sample(values_ref[m])
        back = [pltpu.roll(x, sub - 2, 0) for x in front]
        a0 = front[colours]
        a1 = back[colours]
        colour = [a0 * front[c] for c in range(colours)]
        transmit = 1.0 - a0
        weight = transmit * a1
        colour = [colour[c] + weight * back[c] for c in range(colours)]
        transmit = transmit * (1.0 - a1)
        part = colour + [1.0 - transmit]
        for e in range(2):
            brick = 2 * m + e
            place = (brick // members) * members + order_ref[brick // members, brick % members]
            for c in range(colours + 1):
                parts_ref[c, place] = part[c] if e == 0 else pltpu.roll(part[c], sub - 4, 0)
        return carry

    lax.fori_loop(0, tiles, shade, 0, unroll=32)

    def blend(k, pics):
        out = []
        for g in range(groups):
            pic = pics[g]
            clear = 1.0 - pic[colours]
            out.append(tuple(pic[c] + clear * parts_ref[c, g * members + k] for c in range(colours + 1)))
        return tuple(out)

    zero = jnp.zeros((sub, lanes), jnp.float32)
    start = tuple(tuple(zero for _ in range(colours + 1)) for _ in range(groups))
    pics = lax.fori_loop(0, members, blend, start, unroll=8)
    final = pics[0]
    for g in range(1, groups):
        clear = 1.0 - final[colours]
        final = tuple(final[c] + clear * pics[g][c] for c in range(colours + 1))
    for c in range(colours + 1):
        for j in range(2):
            out_ref[c : c + 1, j * lanes : (j + 1) * lanes] = final[c][j : j + 1]


def render(arrived, colour_table, opacity_table, depth_order):
    devices = arrived.shape[0]
    groups, members = depth_order.shape
    lanes = arrived.shape[2]
    sub = 2 * arrived.shape[1]
    tiles = arrived.reshape(devices // 2, sub, lanes)
    channels = colour_table.shape[0] + 1
    vmem = pl.BlockSpec(memory_space=pltpu.VMEM)
    return pl.pallas_call(
        functools.partial(render_kernel, members),
        out_shape=jax.ShapeDtypeStruct((channels, 2 * lanes), jnp.float32),
        in_specs=[vmem, vmem, vmem, pl.BlockSpec(memory_space=pltpu.SMEM)],
        out_specs=vmem,
        scratch_shapes=[pltpu.VMEM((channels, devices, sub, lanes), jnp.float32)],
    )(tiles, colour_table, opacity_table.reshape(1, -1), depth_order)


def exchange_kernel(bricks_ref, out_ref, send_ref, landed, send_sem, recv_sem, own_sem, arrange_sems):
    devices, chunk, lanes = landed.shape
    depth, height, width = bricks_ref.shape
    per_row = send_ref.shape[1]
    parts = width // per_row // lanes
    members = lax.axis_size("tile")
    me = lax.axis_index("grp") * members + lax.axis_index("tile")

    groups = devices // members
    g = lax.axis_index("grp")
    t = lax.axis_index("tile")

    def peer(k):
        return lax.rem(g + k % groups, groups), lax.rem(t + k // groups, members)

    barrier = pltpu.get_barrier_semaphore()

    def greet(k, carry):
        pl.semaphore_signal(barrier, 1, device_id=peer(k), device_id_type=pl.DeviceIdType.MESH)
        return carry

    lax.fori_loop(1, devices, greet, 0)
    arranging = []
    for s in range(depth):
        for col in range(width // lanes):
            h, j = divmod(col, parts)
            copy = pltpu.make_async_copy(
                bricks_ref.at[s, :, pl.ds(col * lanes, lanes)],
                send_ref.at[:, h, s * parts + j, :],
                arrange_sems.at[len(arranging)],
            )
            copy.start()
            arranging.append(copy)
    for copy in arranging:
        copy.wait()
    pl.semaphore_wait(barrier, devices - 1)

    def send(k, carry):
        peer_g, peer_t = peer(k)
        dest = peer_g * members + peer_t
        pltpu.make_async_remote_copy(
            src_ref=send_ref.at[dest // per_row, dest % per_row],
            dst_ref=landed.at[me],
            send_sem=send_sem,
            recv_sem=recv_sem,
            device_id=(peer_g, peer_t),
            device_id_type=pl.DeviceIdType.MESH,
        ).start()
        return carry

    lax.fori_loop(1, devices, send, 0)
    own = pltpu.make_async_copy(send_ref.at[me // per_row, me % per_row], landed.at[me], own_sem)
    own.start()
    own.wait()
    everything = pltpu.make_async_remote_copy(
        src_ref=landed.at[pl.ds(0, devices - 1)],
        dst_ref=landed.at[pl.ds(0, devices - 1)],
        send_sem=send_sem,
        recv_sem=recv_sem,
        device_id=(me // members, me % members),
        device_id_type=pl.DeviceIdType.MESH,
    )
    everything.wait_send()
    everything.wait_recv()
    out_ref[...] = landed[...]


def exchange(bricks, devices):
    depth, height, width = bricks.shape
    block = height * width // devices
    per_row = width // block
    chunk = depth * block // LANES
    shape = (devices, chunk, LANES)
    return pl.pallas_call(
        exchange_kernel,
        out_shape=jax.ShapeDtypeStruct(shape, bricks.dtype),
        in_specs=[pl.BlockSpec(memory_space=pltpu.VMEM)],
        out_specs=pl.BlockSpec(memory_space=pltpu.VMEM),
        scratch_shapes=[
            pltpu.VMEM((height, per_row, chunk, LANES), bricks.dtype),
            pltpu.VMEM(shape, bricks.dtype),
            pltpu.SemaphoreType.DMA,
            pltpu.SemaphoreType.DMA,
            pltpu.SemaphoreType.DMA,
            pltpu.SemaphoreType.DMA((depth * width // LANES,)),
        ],
        compiler_params=pltpu.CompilerParams(collective_id=0, has_side_effects=True),
    )(bricks)


def body(bricks, colour_table, opacity_table, depth_order):
    groups = lax.axis_size("grp")
    members = lax.axis_size("tile")
    devices = groups * members
    arrived = exchange(bricks, devices)
    return render(arrived, colour_table, opacity_table, depth_order)


def solution(mesh):
    in_specs = (P(("grp", "tile"), None, None), P(), P(), P())
    out_specs = P(None, ("grp", "tile"))
    return jax.shard_map(body, mesh=mesh, in_specs=in_specs, out_specs=out_specs, check_vma=False)
```

```python
import functools

import jax
import jax.numpy as jnp
from jax import lax
from jax.experimental import pallas as pl
from jax.experimental.pallas import tpu as pltpu
from jax.sharding import PartitionSpec as P

LANES = 128


def render_kernel(members, values_ref, colour_ref, opacity_ref, order_ref, out_ref, parts_ref):
    tiles, sub, lanes = values_ref.shape
    knots = colour_ref.shape[1]
    halves = knots // lanes
    colours = colour_ref.shape[0]
    groups = parts_ref.shape[1] // members
    rows = [colour_ref[c : c + 1, :] for c in range(colours)] + [opacity_ref[...]]
    tables = [
        [jnp.broadcast_to(r[:, h * lanes : (h + 1) * lanes], (sub, lanes)) for h in range(halves)]
        for r in rows
    ]
    last_lane = lax.broadcasted_iota(jnp.int32, (sub, lanes), 1) == lanes - 1
    uppers = []
    for per_half in tables:
        shifted = [pltpu.roll(x, lanes - 1, 1) for x in per_half]
        uppers.append(
            [jnp.where(last_lane, shifted[h + 1], shifted[h]) if h + 1 < halves else shifted[h] for h in range(halves)]
        )

    def pick(table, lane, in_half):
        got = jnp.take_along_axis(table[0], lane, axis=1, mode="promise_in_bounds")
        for h in range(1, halves):
            other = jnp.take_along_axis(table[h], lane, axis=1, mode="promise_in_bounds")
            got = jnp.where(in_half[h], other, got)
        return got

    def sample(v):
        u = v * float(knots - 1)
        lower = jnp.clip(jnp.floor(u), 0.0, float(knots - 2))
        frac = u - lower
        index = lower.astype(jnp.int32)
        lane = index % lanes
        half = index // lanes
        in_half = [None] + [half == h for h in range(1, halves)]
        return [
            pick(tables[c], lane, in_half) * (1.0 - frac) + pick(uppers[c], lane, in_half) * frac
            for c in range(colours + 1)
        ]

    def shade(m, carry):
        front = sample(values_ref[m])
        back = [pltpu.roll(x, sub - 2, 0) for x in front]
        a0 = front[colours]
        a1 = back[colours]
        colour = [a0 * front[c] for c in range(colours)]
        transmit = 1.0 - a0
        weight = transmit * a1
        colour = [colour[c] + weight * back[c] for c in range(colours)]
        transmit = transmit * (1.0 - a1)
        part = colour + [1.0 - transmit]
        for e in range(2):
            brick = 2 * m + e
            place = (brick // members) * members + order_ref[brick // members, brick % members]
            for c in range(colours + 1):
                parts_ref[c, place] = part[c] if e == 0 else pltpu.roll(part[c], sub - 4, 0)
        return carry

    lax.fori_loop(0, tiles, shade, 0, unroll=32)

    def blend(k, pics):
        out = []
        for g in range(groups):
            pic = pics[g]
            clear = 1.0 - pic[colours]
            out.append(tuple(pic[c] + clear * parts_ref[c, g * members + k] for c in range(colours + 1)))
        return tuple(out)

    zero = jnp.zeros((sub, lanes), jnp.float32)
    start = tuple(tuple(zero for _ in range(colours + 1)) for _ in range(groups))
    pics = lax.fori_loop(0, members, blend, start, unroll=8)
    final = pics[0]
    for g in range(1, groups):
        clear = 1.0 - final[colours]
        final = tuple(final[c] + clear * pics[g][c] for c in range(colours + 1))
    for c in range(colours + 1):
        for j in range(2):
            out_ref[c : c + 1, j * lanes : (j + 1) * lanes] = final[c][j : j + 1]


def render(arrived, colour_table, opacity_table, depth_order):
    devices = arrived.shape[0]
    groups, members = depth_order.shape
    lanes = arrived.shape[2]
    sub = 2 * arrived.shape[1]
    tiles = arrived.reshape(devices // 2, sub, lanes)
    channels = colour_table.shape[0] + 1
    vmem = pl.BlockSpec(memory_space=pltpu.VMEM)
    return pl.pallas_call(
        functools.partial(render_kernel, members),
        out_shape=jax.ShapeDtypeStruct((channels, 2 * lanes), jnp.float32),
        in_specs=[vmem, vmem, vmem, pl.BlockSpec(memory_space=pltpu.SMEM)],
        out_specs=vmem,
        scratch_shapes=[pltpu.VMEM((channels, devices, sub, lanes), jnp.float32)],
    )(tiles, colour_table, opacity_table.reshape(1, -1), depth_order)


def exchange_kernel(bricks_ref, landed, send_ref, send_sem, recv_sem, own_sem, arrange_sems):
    devices, chunk, lanes = landed.shape
    depth, height, width = bricks_ref.shape
    per_row = send_ref.shape[1]
    parts = width // per_row // lanes
    members = lax.axis_size("tile")
    me = lax.axis_index("grp") * members + lax.axis_index("tile")

    groups = devices // members
    g = lax.axis_index("grp")
    t = lax.axis_index("tile")

    def peer(k):
        return lax.rem(g + k % groups, groups), lax.rem(t + k // groups, members)

    barrier = pltpu.get_barrier_semaphore()

    def greet(k, carry):
        pl.semaphore_signal(barrier, 1, device_id=peer(k), device_id_type=pl.DeviceIdType.MESH)
        return carry

    lax.fori_loop(1, devices, greet, 0)
    arranging = []
    for s in range(depth):
        for col in range(width // lanes):
            h, j = divmod(col, parts)
            copy = pltpu.make_async_copy(
                bricks_ref.at[s, :, pl.ds(col * lanes, lanes)],
                send_ref.at[:, h, s * parts + j, :],
                arrange_sems.at[len(arranging)],
            )
            copy.start()
            arranging.append(copy)
    for copy in arranging:
        copy.wait()
    pl.semaphore_wait(barrier, devices - 1)

    def send(k, carry):
        peer_g, peer_t = peer(k)
        dest = peer_g * members + peer_t
        pltpu.make_async_remote_copy(
            src_ref=send_ref.at[dest // per_row, dest % per_row],
            dst_ref=landed.at[me],
            send_sem=send_sem,
            recv_sem=recv_sem,
            device_id=(peer_g, peer_t),
            device_id_type=pl.DeviceIdType.MESH,
        ).start()
        return carry

    lax.fori_loop(1, devices, send, 0)
    own = pltpu.make_async_copy(send_ref.at[me // per_row, me % per_row], landed.at[me], own_sem)
    own.start()
    own.wait()
    everything = pltpu.make_async_remote_copy(
        src_ref=landed.at[pl.ds(0, devices - 1)],
        dst_ref=landed.at[pl.ds(0, devices - 1)],
        send_sem=send_sem,
        recv_sem=recv_sem,
        device_id=(me // members, me % members),
        device_id_type=pl.DeviceIdType.MESH,
    )
    everything.wait_send()
    everything.wait_recv()


def exchange(bricks, devices):
    depth, height, width = bricks.shape
    block = height * width // devices
    per_row = width // block
    chunk = depth * block // LANES
    shape = (devices, chunk, LANES)
    return pl.pallas_call(
        exchange_kernel,
        out_shape=jax.ShapeDtypeStruct(shape, bricks.dtype),
        in_specs=[pl.BlockSpec(memory_space=pltpu.VMEM)],
        out_specs=pl.BlockSpec(memory_space=pltpu.VMEM),
        scratch_shapes=[
            pltpu.VMEM((height, per_row, chunk, LANES), bricks.dtype),
            pltpu.SemaphoreType.DMA,
            pltpu.SemaphoreType.DMA,
            pltpu.SemaphoreType.DMA,
            pltpu.SemaphoreType.DMA((depth * width // LANES,)),
        ],
        compiler_params=pltpu.CompilerParams(collective_id=0, has_side_effects=True),
    )(bricks)


def body(bricks, colour_table, opacity_table, depth_order):
    groups = lax.axis_size("grp")
    members = lax.axis_size("tile")
    devices = groups * members
    arrived = exchange(bricks, devices)
    return render(arrived, colour_table, opacity_table, depth_order)


def solution(mesh):
    in_specs = (P(("grp", "tile"), None, None), P(), P(), P())
    out_specs = P(None, ("grp", "tile"))
    return jax.shard_map(body, mesh=mesh, in_specs=in_specs, out_specs=out_specs, check_vma=False)
```

```python
import functools

import jax
import jax.numpy as jnp
from jax import lax
from jax.experimental import pallas as pl
from jax.experimental.pallas import tpu as pltpu
from jax.sharding import PartitionSpec as P

LANES = 128


def render_kernel(members, values_ref, colour_ref, opacity_ref, order_ref, out_ref, parts_ref):
    tiles, sub, lanes = values_ref.shape
    knots = colour_ref.shape[1]
    halves = knots // lanes
    colours = colour_ref.shape[0]
    groups = parts_ref.shape[1] // members
    rows = [colour_ref[c : c + 1, :] for c in range(colours)] + [opacity_ref[...]]
    tables = [
        [jnp.broadcast_to(r[:, h * lanes : (h + 1) * lanes], (sub, lanes)) for h in range(halves)]
        for r in rows
    ]
    last_lane = lax.broadcasted_iota(jnp.int32, (sub, lanes), 1) == lanes - 1
    uppers = []
    for per_half in tables:
        shifted = [pltpu.roll(x, lanes - 1, 1) for x in per_half]
        uppers.append(
            [jnp.where(last_lane, shifted[h + 1], shifted[h]) if h + 1 < halves else shifted[h] for h in range(halves)]
        )

    def pick(table, lane, in_half):
        got = jnp.take_along_axis(table[0], lane, axis=1, mode="promise_in_bounds")
        for h in range(1, halves):
            other = jnp.take_along_axis(table[h], lane, axis=1, mode="promise_in_bounds")
            got = jnp.where(in_half[h], other, got)
        return got

    def sample(v):
        u = v * float(knots - 1)
        lower = jnp.clip(jnp.floor(u), 0.0, float(knots - 2))
        frac = u - lower
        index = lower.astype(jnp.int32)
        lane = index % lanes
        half = index // lanes
        in_half = [None] + [half == h for h in range(1, halves)]
        return [
            pick(tables[c], lane, in_half) * (1.0 - frac) + pick(uppers[c], lane, in_half) * frac
            for c in range(colours + 1)
        ]

    def shade(m, carry):
        front = sample(values_ref[m])
        back = [pltpu.roll(x, sub - 2, 0) for x in front]
        a0 = front[colours]
        a1 = back[colours]
        colour = [a0 * front[c] for c in range(colours)]
        transmit = 1.0 - a0
        weight = transmit * a1
        colour = [colour[c] + weight * back[c] for c in range(colours)]
        transmit = transmit * (1.0 - a1)
        part = colour + [1.0 - transmit]
        for e in range(2):
            brick = 2 * m + e
            place = (brick // members) * members + order_ref[brick // members, brick % members]
            for c in range(colours + 1):
                parts_ref[c, place] = part[c] if e == 0 else pltpu.roll(part[c], sub - 4, 0)
        return carry

    lax.fori_loop(0, tiles, shade, 0, unroll=64)

    def blend(k, pics):
        out = []
        for g in range(groups):
            pic = pics[g]
            clear = 1.0 - pic[colours]
            out.append(tuple(pic[c] + clear * parts_ref[c, g * members + k] for c in range(colours + 1)))
        return tuple(out)

    zero = jnp.zeros((sub, lanes), jnp.float32)
    start = tuple(tuple(zero for _ in range(colours + 1)) for _ in range(groups))
    pics = lax.fori_loop(0, members, blend, start, unroll=16)
    final = pics[0]
    for g in range(1, groups):
        clear = 1.0 - final[colours]
        final = tuple(final[c] + clear * pics[g][c] for c in range(colours + 1))
    for c in range(colours + 1):
        for j in range(2):
            out_ref[c : c + 1, j * lanes : (j + 1) * lanes] = final[c][j : j + 1]


def render(arrived, colour_table, opacity_table, depth_order):
    devices = arrived.shape[0]
    groups, members = depth_order.shape
    lanes = arrived.shape[2]
    sub = 2 * arrived.shape[1]
    tiles = arrived.reshape(devices // 2, sub, lanes)
    channels = colour_table.shape[0] + 1
    vmem = pl.BlockSpec(memory_space=pltpu.VMEM)
    return pl.pallas_call(
        functools.partial(render_kernel, members),
        out_shape=jax.ShapeDtypeStruct((channels, 2 * lanes), jnp.float32),
        in_specs=[vmem, vmem, vmem, pl.BlockSpec(memory_space=pltpu.SMEM)],
        out_specs=vmem,
        scratch_shapes=[pltpu.VMEM((channels, devices, sub, lanes), jnp.float32)],
    )(tiles, colour_table, opacity_table.reshape(1, -1), depth_order)


def exchange_kernel(bricks_ref, out_ref, send_ref, landed, send_sem, recv_sem, own_sem, arrange_sems):
    devices, chunk, lanes = landed.shape
    depth, height, width = bricks_ref.shape
    per_row = send_ref.shape[1]
    parts = width // per_row // lanes
    members = lax.axis_size("tile")
    me = lax.axis_index("grp") * members + lax.axis_index("tile")

    groups = devices // members
    g = lax.axis_index("grp")
    t = lax.axis_index("tile")

    def peer(k):
        return lax.rem(g + k % groups, groups), lax.rem(t + k // groups, members)

    barrier = pltpu.get_barrier_semaphore()

    def greet(k, carry):
        pl.semaphore_signal(barrier, 1, device_id=peer(k), device_id_type=pl.DeviceIdType.MESH)
        return carry

    lax.fori_loop(1, devices, greet, 0)
    arranging = []
    for s in range(depth):
        for col in range(width // lanes):
            h, j = divmod(col, parts)
            copy = pltpu.make_async_copy(
                bricks_ref.at[s, :, pl.ds(col * lanes, lanes)],
                send_ref.at[:, h, s * parts + j, :],
                arrange_sems.at[len(arranging)],
            )
            copy.start()
            arranging.append(copy)
    for copy in arranging:
        copy.wait()
    pl.semaphore_wait(barrier, devices - 1)

    def send(k, carry):
        peer_g, peer_t = peer(k)
        dest = peer_g * members + peer_t
        pltpu.make_async_remote_copy(
            src_ref=send_ref.at[dest // per_row, dest % per_row],
            dst_ref=landed.at[me],
            send_sem=send_sem,
            recv_sem=recv_sem,
            device_id=(peer_g, peer_t),
            device_id_type=pl.DeviceIdType.MESH,
        ).start()
        return carry

    lax.fori_loop(1, devices, send, 0)
    own = pltpu.make_async_copy(send_ref.at[me // per_row, me % per_row], landed.at[me], own_sem)
    own.start()
    own.wait()
    everything = pltpu.make_async_remote_copy(
        src_ref=landed.at[pl.ds(0, devices - 1)],
        dst_ref=landed.at[pl.ds(0, devices - 1)],
        send_sem=send_sem,
        recv_sem=recv_sem,
        device_id=(me // members, me % members),
        device_id_type=pl.DeviceIdType.MESH,
    )
    everything.wait_send()
    everything.wait_recv()
    out_ref[...] = landed[...]


def exchange(bricks, devices):
    depth, height, width = bricks.shape
    block = height * width // devices
    per_row = width // block
    chunk = depth * block // LANES
    shape = (devices, chunk, LANES)
    return pl.pallas_call(
        exchange_kernel,
        out_shape=jax.ShapeDtypeStruct(shape, bricks.dtype),
        in_specs=[pl.BlockSpec(memory_space=pltpu.VMEM)],
        out_specs=pl.BlockSpec(memory_space=pltpu.VMEM),
        scratch_shapes=[
            pltpu.VMEM((height, per_row, chunk, LANES), bricks.dtype),
            pltpu.VMEM(shape, bricks.dtype),
            pltpu.SemaphoreType.DMA,
            pltpu.SemaphoreType.DMA,
            pltpu.SemaphoreType.DMA,
            pltpu.SemaphoreType.DMA((depth * width // LANES,)),
        ],
        compiler_params=pltpu.CompilerParams(collective_id=0, has_side_effects=True),
    )(bricks)


def body(bricks, colour_table, opacity_table, depth_order):
    groups = lax.axis_size("grp")
    members = lax.axis_size("tile")
    devices = groups * members
    arrived = exchange(bricks, devices)
    return render(arrived, colour_table, opacity_table, depth_order)


def solution(mesh):
    in_specs = (P(("grp", "tile"), None, None), P(), P(), P())
    out_specs = P(None, ("grp", "tile"))
    return jax.shard_map(body, mesh=mesh, in_specs=in_specs, out_specs=out_specs, check_vma=False)
```

```python
import functools

import jax
import jax.numpy as jnp
from jax import lax
from jax.experimental import pallas as pl
from jax.experimental.pallas import tpu as pltpu
from jax.sharding import PartitionSpec as P

LANES = 128


def render_kernel(members, values_ref, colour_ref, opacity_ref, order_ref, out_ref, parts_ref):
    tiles, sub, lanes = values_ref.shape
    knots = colour_ref.shape[1]
    halves = knots // lanes
    colours = colour_ref.shape[0]
    groups = parts_ref.shape[1] // members
    rows = [colour_ref[c : c + 1, :] for c in range(colours)] + [opacity_ref[...]]
    tables = [
        [jnp.broadcast_to(r[:, h * lanes : (h + 1) * lanes], (sub, lanes)) for h in range(halves)]
        for r in rows
    ]
    last_lane = lax.broadcasted_iota(jnp.int32, (sub, lanes), 1) == lanes - 1
    uppers = []
    for per_half in tables:
        shifted = [pltpu.roll(x, lanes - 1, 1) for x in per_half]
        uppers.append(
            [jnp.where(last_lane, shifted[h + 1], shifted[h]) if h + 1 < halves else shifted[h] for h in range(halves)]
        )

    def pick(table, lane, in_half):
        got = jnp.take_along_axis(table[0], lane, axis=1, mode="promise_in_bounds")
        for h in range(1, halves):
            other = jnp.take_along_axis(table[h], lane, axis=1, mode="promise_in_bounds")
            got = jnp.where(in_half[h], other, got)
        return got

    def sample(v):
        u = v * float(knots - 1)
        lower = jnp.clip(jnp.floor(u), 0.0, float(knots - 2))
        frac = u - lower
        index = lower.astype(jnp.int32)
        lane = index % lanes
        half = index // lanes
        in_half = [None] + [half == h for h in range(1, halves)]
        return [
            pick(tables[c], lane, in_half) * (1.0 - frac) + pick(uppers[c], lane, in_half) * frac
            for c in range(colours + 1)
        ]

    def shade(m, carry):
        front = sample(values_ref[m])
        back = [pltpu.roll(x, sub - 2, 0) for x in front]
        a0 = front[colours]
        a1 = back[colours]
        colour = [a0 * front[c] for c in range(colours)]
        transmit = 1.0 - a0
        weight = transmit * a1
        colour = [colour[c] + weight * back[c] for c in range(colours)]
        transmit = transmit * (1.0 - a1)
        part = colour + [1.0 - transmit]
        for e in range(2):
            brick = 2 * m + e
            place = (brick // members) * members + order_ref[brick // members, brick % members]
            for c in range(colours + 1):
                parts_ref[c, place] = part[c] if e == 0 else pltpu.roll(part[c], sub - 4, 0)
        return carry

    lax.fori_loop(0, tiles, shade, 0, unroll=64)

    def blend(k, pics):
        out = []
        for g in range(groups):
            pic = pics[g]
            clear = 1.0 - pic[colours]
            out.append(tuple(pic[c] + clear * parts_ref[c, g * members + k] for c in range(colours + 1)))
        return tuple(out)

    zero = jnp.zeros((sub, lanes), jnp.float32)
    start = tuple(tuple(zero for _ in range(colours + 1)) for _ in range(groups))
    pics = lax.fori_loop(0, members, blend, start, unroll=16)
    final = pics[0]
    for g in range(1, groups):
        clear = 1.0 - final[colours]
        final = tuple(final[c] + clear * pics[g][c] for c in range(colours + 1))
    for c in range(colours + 1):
        for j in range(2):
            out_ref[c : c + 1, j * lanes : (j + 1) * lanes] = final[c][j : j + 1]


def render(arrived, colour_table, opacity_table, depth_order):
    devices = arrived.shape[0]
    groups, members = depth_order.shape
    lanes = arrived.shape[2]
    sub = 2 * arrived.shape[1]
    tiles = arrived.reshape(devices // 2, sub, lanes)
    channels = colour_table.shape[0] + 1
    vmem = pl.BlockSpec(memory_space=pltpu.VMEM)
    return pl.pallas_call(
        functools.partial(render_kernel, members),
        out_shape=jax.ShapeDtypeStruct((channels, 2 * lanes), jnp.float32),
        in_specs=[vmem, vmem, vmem, pl.BlockSpec(memory_space=pltpu.SMEM)],
        out_specs=vmem,
        scratch_shapes=[pltpu.VMEM((channels, devices, sub, lanes), jnp.float32)],
    )(tiles, colour_table, opacity_table.reshape(1, -1), depth_order)


def exchange_kernel(bricks_ref, out_ref, send_ref, landed, send_sem, recv_sem, own_sem, arrange_sems):
    devices, chunk, lanes = landed.shape
    depth, height, width = bricks_ref.shape
    per_row = send_ref.shape[1]
    parts = width // per_row // lanes
    members = lax.axis_size("tile")
    me = lax.axis_index("grp") * members + lax.axis_index("tile")

    groups = devices // members
    g = lax.axis_index("grp")
    t = lax.axis_index("tile")

    def peer(k):
        return lax.rem(g + k % groups, groups), lax.rem(t + k // groups, members)

    barrier = pltpu.get_barrier_semaphore()

    def greet(k, carry):
        pl.semaphore_signal(barrier, 1, device_id=peer(devices - k), device_id_type=pl.DeviceIdType.MESH)
        return carry

    lax.fori_loop(1, devices, greet, 0)
    arranging = []
    for s in range(depth):
        for col in range(width // lanes):
            h, j = divmod(col, parts)
            copy = pltpu.make_async_copy(
                bricks_ref.at[s, :, pl.ds(col * lanes, lanes)],
                send_ref.at[:, h, s * parts + j, :],
                arrange_sems.at[len(arranging)],
            )
            copy.start()
            arranging.append(copy)
    for copy in arranging:
        copy.wait()
    pl.semaphore_wait(barrier, devices - 1)

    def send(k, carry):
        peer_g, peer_t = peer(k)
        dest = peer_g * members + peer_t
        pltpu.make_async_remote_copy(
            src_ref=send_ref.at[dest // per_row, dest % per_row],
            dst_ref=landed.at[me],
            send_sem=send_sem,
            recv_sem=recv_sem,
            device_id=(peer_g, peer_t),
            device_id_type=pl.DeviceIdType.MESH,
        ).start()
        return carry

    lax.fori_loop(1, devices, send, 0)
    own = pltpu.make_async_copy(send_ref.at[me // per_row, me % per_row], landed.at[me], own_sem)
    own.start()
    own.wait()
    everything = pltpu.make_async_remote_copy(
        src_ref=landed.at[pl.ds(0, devices - 1)],
        dst_ref=landed.at[pl.ds(0, devices - 1)],
        send_sem=send_sem,
        recv_sem=recv_sem,
        device_id=(me // members, me % members),
        device_id_type=pl.DeviceIdType.MESH,
    )
    everything.wait_send()
    everything.wait_recv()
    out_ref[...] = landed[...]


def exchange(bricks, devices):
    depth, height, width = bricks.shape
    block = height * width // devices
    per_row = width // block
    chunk = depth * block // LANES
    shape = (devices, chunk, LANES)
    return pl.pallas_call(
        exchange_kernel,
        out_shape=jax.ShapeDtypeStruct(shape, bricks.dtype),
        in_specs=[pl.BlockSpec(memory_space=pltpu.VMEM)],
        out_specs=pl.BlockSpec(memory_space=pltpu.VMEM),
        scratch_shapes=[
            pltpu.VMEM((height, per_row, chunk, LANES), bricks.dtype),
            pltpu.VMEM(shape, bricks.dtype),
            pltpu.SemaphoreType.DMA,
            pltpu.SemaphoreType.DMA,
            pltpu.SemaphoreType.DMA,
            pltpu.SemaphoreType.DMA((depth * width // LANES,)),
        ],
        compiler_params=pltpu.CompilerParams(collective_id=0, has_side_effects=True),
    )(bricks)


def body(bricks, colour_table, opacity_table, depth_order):
    groups = lax.axis_size("grp")
    members = lax.axis_size("tile")
    devices = groups * members
    arrived = exchange(bricks, devices)
    return render(arrived, colour_table, opacity_table, depth_order)


def solution(mesh):
    in_specs = (P(("grp", "tile"), None, None), P(), P(), P())
    out_specs = P(None, ("grp", "tile"))
    return jax.shard_map(body, mesh=mesh, in_specs=in_specs, out_specs=out_specs, check_vma=False)
```

```python
import functools

import jax
import jax.numpy as jnp
from jax import lax
from jax.experimental import pallas as pl
from jax.experimental.pallas import tpu as pltpu
from jax.sharding import PartitionSpec as P

LANES = 128


def render_kernel(members, values_ref, colour_ref, opacity_ref, order_ref, out_ref, parts_ref):
    tiles, sub, lanes = values_ref.shape
    knots = colour_ref.shape[1]
    halves = knots // lanes
    colours = colour_ref.shape[0]
    groups = parts_ref.shape[1] // members
    rows = [colour_ref[c : c + 1, :] for c in range(colours)] + [opacity_ref[...]]
    tables = [
        [jnp.broadcast_to(r[:, h * lanes : (h + 1) * lanes], (sub, lanes)) for h in range(halves)]
        for r in rows
    ]
    last_lane = lax.broadcasted_iota(jnp.int32, (sub, lanes), 1) == lanes - 1
    uppers = []
    for per_half in tables:
        shifted = [pltpu.roll(x, lanes - 1, 1) for x in per_half]
        uppers.append(
            [jnp.where(last_lane, shifted[h + 1], shifted[h]) if h + 1 < halves else shifted[h] for h in range(halves)]
        )

    def pick(table, lane, in_half):
        got = jnp.take_along_axis(table[0], lane, axis=1, mode="promise_in_bounds")
        for h in range(1, halves):
            other = jnp.take_along_axis(table[h], lane, axis=1, mode="promise_in_bounds")
            got = jnp.where(in_half[h], other, got)
        return got

    def sample(v):
        u = v * float(knots - 1)
        lower = jnp.clip(jnp.floor(u), 0.0, float(knots - 2))
        frac = u - lower
        index = lower.astype(jnp.int32)
        lane = index % lanes
        half = index // lanes
        in_half = [None] + [half == h for h in range(1, halves)]
        return [
            pick(tables[c], lane, in_half) * (1.0 - frac) + pick(uppers[c], lane, in_half) * frac
            for c in range(colours + 1)
        ]

    def shade(m, carry):
        front = sample(values_ref[m])
        back = [pltpu.roll(x, sub - 2, 0) for x in front]
        a0 = front[colours]
        a1 = back[colours]
        colour = [a0 * front[c] for c in range(colours)]
        transmit = 1.0 - a0
        weight = transmit * a1
        colour = [colour[c] + weight * back[c] for c in range(colours)]
        transmit = transmit * (1.0 - a1)
        part = colour + [1.0 - transmit]
        for e in range(2):
            brick = 2 * m + e
            place = (brick // members) * members + order_ref[brick // members, brick % members]
            for c in range(colours + 1):
                parts_ref[c, place] = part[c] if e == 0 else pltpu.roll(part[c], sub - 4, 0)
        return carry

    lax.fori_loop(0, tiles, shade, 0, unroll=128)

    def blend(k, pics):
        out = []
        for g in range(groups):
            pic = pics[g]
            clear = 1.0 - pic[colours]
            out.append(tuple(pic[c] + clear * parts_ref[c, g * members + k] for c in range(colours + 1)))
        return tuple(out)

    zero = jnp.zeros((sub, lanes), jnp.float32)
    start = tuple(tuple(zero for _ in range(colours + 1)) for _ in range(groups))
    pics = lax.fori_loop(0, members, blend, start, unroll=64)
    final = pics[0]
    for g in range(1, groups):
        clear = 1.0 - final[colours]
        final = tuple(final[c] + clear * pics[g][c] for c in range(colours + 1))
    for c in range(colours + 1):
        for j in range(2):
            out_ref[c : c + 1, j * lanes : (j + 1) * lanes] = final[c][j : j + 1]


def render(arrived, colour_table, opacity_table, depth_order):
    devices = arrived.shape[0]
    groups, members = depth_order.shape
    lanes = arrived.shape[2]
    sub = 2 * arrived.shape[1]
    tiles = arrived.reshape(devices // 2, sub, lanes)
    channels = colour_table.shape[0] + 1
    vmem = pl.BlockSpec(memory_space=pltpu.VMEM)
    return pl.pallas_call(
        functools.partial(render_kernel, members),
        out_shape=jax.ShapeDtypeStruct((channels, 2 * lanes), jnp.float32),
        in_specs=[vmem, vmem, vmem, pl.BlockSpec(memory_space=pltpu.SMEM)],
        out_specs=vmem,
        scratch_shapes=[pltpu.VMEM((channels, devices, sub, lanes), jnp.float32)],
    )(tiles, colour_table, opacity_table.reshape(1, -1), depth_order)


def exchange_kernel(bricks_ref, out_ref, send_ref, landed, send_sem, recv_sem, own_sem, arrange_sems):
    devices, chunk, lanes = landed.shape
    depth, height, width = bricks_ref.shape
    per_row = send_ref.shape[1]
    parts = width // per_row // lanes
    members = lax.axis_size("tile")
    me = lax.axis_index("grp") * members + lax.axis_index("tile")

    groups = devices // members
    g = lax.axis_index("grp")
    t = lax.axis_index("tile")

    def peer(k):
        return lax.rem(g + k % groups, groups), lax.rem(t + k // groups, members)

    barrier = pltpu.get_barrier_semaphore()

    def greet(k, carry):
        pl.semaphore_signal(barrier, 1, device_id=peer(k), device_id_type=pl.DeviceIdType.MESH)
        return carry

    lax.fori_loop(1, devices, greet, 0)
    arranging = []
    for s in range(depth):
        for col in range(width // lanes):
            h, j = divmod(col, parts)
            copy = pltpu.make_async_copy(
                bricks_ref.at[s, :, pl.ds(col * lanes, lanes)],
                send_ref.at[:, h, s * parts + j, :],
                arrange_sems.at[len(arranging)],
            )
            copy.start()
            arranging.append(copy)
    for copy in arranging:
        copy.wait()
    pl.semaphore_wait(barrier, devices - 1)

    def send(k, carry):
        peer_g, peer_t = peer(k)
        dest = peer_g * members + peer_t
        pltpu.make_async_remote_copy(
            src_ref=send_ref.at[dest // per_row, dest % per_row],
            dst_ref=landed.at[me],
            send_sem=send_sem,
            recv_sem=recv_sem,
            device_id=(peer_g, peer_t),
            device_id_type=pl.DeviceIdType.MESH,
        ).start()
        return carry

    lax.fori_loop(1, devices, send, 0)
    own = pltpu.make_async_copy(send_ref.at[me // per_row, me % per_row], landed.at[me], own_sem)
    own.start()
    own.wait()
    everything = pltpu.make_async_remote_copy(
        src_ref=landed.at[pl.ds(0, devices - 1)],
        dst_ref=landed.at[pl.ds(0, devices - 1)],
        send_sem=send_sem,
        recv_sem=recv_sem,
        device_id=(me // members, me % members),
        device_id_type=pl.DeviceIdType.MESH,
    )
    everything.wait_send()
    everything.wait_recv()
    out_ref[...] = landed[...]


def exchange(bricks, devices):
    depth, height, width = bricks.shape
    block = height * width // devices
    per_row = width // block
    chunk = depth * block // LANES
    shape = (devices, chunk, LANES)
    return pl.pallas_call(
        exchange_kernel,
        out_shape=jax.ShapeDtypeStruct(shape, bricks.dtype),
        in_specs=[pl.BlockSpec(memory_space=pltpu.VMEM)],
        out_specs=pl.BlockSpec(memory_space=pltpu.VMEM),
        scratch_shapes=[
            pltpu.VMEM((height, per_row, chunk, LANES), bricks.dtype),
            pltpu.VMEM(shape, bricks.dtype),
            pltpu.SemaphoreType.DMA,
            pltpu.SemaphoreType.DMA,
            pltpu.SemaphoreType.DMA,
            pltpu.SemaphoreType.DMA((depth * width // LANES,)),
        ],
        compiler_params=pltpu.CompilerParams(collective_id=0, has_side_effects=True),
    )(bricks)


def body(bricks, colour_table, opacity_table, depth_order):
    groups = lax.axis_size("grp")
    members = lax.axis_size("tile")
    devices = groups * members
    arrived = exchange(bricks, devices)
    return render(arrived, colour_table, opacity_table, depth_order)


def solution(mesh):
    in_specs = (P(("grp", "tile"), None, None), P(), P(), P())
    out_specs = P(None, ("grp", "tile"))
    return jax.shard_map(body, mesh=mesh, in_specs=in_specs, out_specs=out_specs, check_vma=False)
```
